32 devices in a mesh: shard: 8 (over y, x, core), tensor: 4 (over z).
Axes of the slice: x: 2, y: 2, z: 4, core: 2. Of those that a mesh axis runs over, the one named last changes fastest.
Arguments:
- step: int32 [1], replicated, may hold values from 1 to 19
- lengths: int32 [80], replicated, may hold values from 1 to 262144, 2097152 in all
- grads: bfloat16 [8, 8, 4, 65536], P('shard', None, 'tensor'), may hold values from -2 to 2
- weights: float32 [2097152], P(('shard', 'tensor'))
- moment1: float32 [2097152], P(('shard', 'tensor')), may hold values from -0.4375 to 0.4375
- moment2: float32 [2097152], P(('shard', 'tensor')), may hold values from 0.0001 to 0.01
Outputs:
- new_weights: float32 [2097152], P(('shard', 'tensor'))
- new_moment1: float32 [2097152], P(('shard', 'tensor'))
- new_moment2: float32 [2097152], P(('shard', 'tensor'))
- train_weights: bfloat16 [8, 4, 65536], P(None, 'tensor')
The draws below stay inside these ranges and needn't reach their ends.
Inputs may be any that keep to these rules, and one draw needn't show every extreme that they name: The lengths sum to 2097152, and one of them equals 262144.
All inputs are finite; a program needn't handle non-finite values.
Results may differ from the reference program's by a relative error of at most 0.0004.
Values may be sent and summed in bfloat16 or wider, within the bound.
No kernel may reach another device: no remote copies, remote signals or barrier semaphores. Data moves between devices by JAX's collectives and lax.ppermute only.
A program may use at most 128 MiB of HBM per device.

```python
import math
import jax
import jax.numpy as jnp
import numpy as np
from jax import lax

P_DEV = 65536
NT = 80
FLAT = 2097152
MOST_LEN = 262144
N_SHARD = 8
N_TENSOR = 4


def draw_weights(key, part):
    position = jnp.arange(FLAT, dtype=jnp.float32) / FLAT
    rising = jnp.power(jnp.float32(3.0), position)
    return (jax.random.normal(key, (FLAT,), jnp.float32) * rising).astype(jnp.float32)


def raised(values, stream_key, source, target, shards_of, factor):
    owner, partner = [(jnp.arange(values.shape[dim]) // (values.shape[dim] // shards_of)).reshape([-1 if axis == dim else 1 for axis in range(values.ndim)]) for dim in (source, target)]
    chosen = jax.random.permutation(stream_key, shards_of)[partner]
    strong = (owner == chosen) | (owner == (partner + shards_of // 2) % shards_of)
    return jnp.where(strong, factor * values, values)


def shard_levels(stream_key, dims, cuts, least, largest):
    level, own = 1.0, jax.random.fold_in(stream_key, 6)
    for axis_at, parts in cuts:
        heights = jnp.exp(jax.random.uniform(jax.random.fold_in(own, axis_at), (parts,), jnp.float32, least / len(cuts), largest / len(cuts)))
        level = level * jnp.repeat(heights, dims[axis_at] // parts).reshape([-1 if axis == axis_at else 1 for axis in range(len(dims))])
    return level


def split_up(amount, total, limit, skew):
    loads = [(1 << 20) // math.isqrt(grade ** skew) + 1 for grade in range(2, amount + 1)]
    surplus, given = total - limit - (amount - 1), [1] * (amount - 1)
    while surplus > 0:
        candidates = [i for i in range(amount - 1) if given[i] < limit]
        pool, remaining = sum([loads[i] for i in candidates]), surplus
        for i in candidates:
            addition = min(limit - given[i], max(1, remaining * loads[i] // pool), surplus)
            given[i] = given[i] + addition
            surplus = surplus - addition
    return np.array([limit] + given)


def ragged(own_key, number_of, total, most, slope):
    if number_of == 2:
        one = jax.random.randint(own_key, (), max(1, total - most), min(most, total - 1) + 1)
        return jnp.stack([one, total - one])
    tallies = jnp.asarray(split_up(number_of, total, most, slope), jnp.int32)
    pairs = (number_of - 1) // 2
    source_of, taker = tallies[1:1 + 2 * pairs:2], tallies[2:2 + 2 * pairs:2]
    slack = jnp.minimum(source_of - 1, most - taker)
    passed = jax.random.randint(jax.random.fold_in(own_key, 1), (pairs,), 0, 1 << 20) % (slack + 1)
    tallies = tallies.at[1:1 + 2 * pairs:2].set(source_of - passed).at[2:2 + 2 * pairs:2].set(taker + passed)
    return tallies[jax.random.permutation(jax.random.fold_in(own_key, 2), number_of)]


def normal_values(key, shape, spread, reach, pieces=(), kind=jnp.bfloat16):
    array = spread * jax.random.normal(key, shape, jnp.float32)
    if pieces:
        array = array * shard_levels(key, shape, pieces, -0.22, 0.18)
    return jnp.clip(array, -reach, reach).astype(kind)


def gaussian_with(rng, dims, scale, limit, cuts, heavy, kind=jnp.bfloat16):
    entries = scale * jax.random.normal(rng, dims, jnp.float32)
    if cuts:
        entries = entries * shard_levels(rng, dims, cuts, -0.22, 0.18)
    return jnp.clip(raised(entries, jax.random.fold_in(rng, 3), *heavy), -limit, limit).astype(kind)


def setup_inputs(seed: int = 0) -> dict:
    key_list = jax.random.split(jax.random.key(seed), 7)
    step = jax.random.randint(key_list[0], (1,), 1, 20).astype(jnp.int32)
    lengths = ragged(key_list[1], NT, FLAT, MOST_LEN, 1).astype(jnp.int32)
    grads = gaussian_with(key_list[2], (N_SHARD, N_SHARD, N_TENSOR, P_DEV), 0.1, 2.0, ((0, 8), (2, 4)), (0, 1, 8, 2.0))
    weights = draw_weights(jax.random.fold_in(key_list[6], 71), 0)
    moment1 = normal_values(key_list[4], (FLAT,), 0.03, 0.4375, ((0, 32),), jnp.float32)
    moment2 = jnp.clip(jnp.exp(math.log(0.01) - 4.6051702 * jax.random.uniform(key_list[5], (FLAT,), jnp.float32) ** shard_levels(key_list[5], (FLAT,), ((0, 32),), -0.2, 0.2)), 0.0001, 0.01)
    return dict(step=step, lengths=lengths, grads=grads, weights=weights, moment1=moment1, moment2=moment2)


def reference(step, lengths, grads, weights, moment1, moment2):
    zeros = jnp.zeros((N_SHARD, N_TENSOR, P_DEV), jnp.float32)

    def accumulate(total, piece):
        return (total + piece.astype(jnp.float32), None)
    summed, unused = lax.scan(accumulate, zeros, grads)
    grad = summed.reshape(-1)
    ends = jnp.cumsum(lengths).astype(jnp.int32)
    position = jnp.arange(FLAT, dtype=jnp.int32)
    seg = jnp.searchsorted(ends, position, side='right').astype(jnp.int32)
    seg = jnp.minimum(seg, NT - 1)
    count = step[0].astype(jnp.float32)
    first = 1.0 - jnp.power(jnp.float32(0.9), count)
    second = 1.0 - jnp.power(jnp.float32(0.999), count)
    new_moment1 = 0.9 * moment1 + 0.1 * grad
    new_moment2 = 0.999 * moment2 + 0.001 * grad * grad
    update = new_moment1 / first / (jnp.sqrt(new_moment2 / second) + 1e-06) + 0.1 * weights
    wsq = jax.ops.segment_sum(weights * weights, seg, NT)
    usq = jax.ops.segment_sum(update * update, seg, NT)
    ratio = jnp.sqrt(wsq) / jnp.maximum(jnp.sqrt(usq), 1.0)
    new_weights = weights - 0.25 * ratio[seg] * update
    train_weights = new_weights.astype(jnp.bfloat16).reshape(N_SHARD, N_TENSOR, P_DEV)
    return (new_weights, new_moment1, new_moment2, train_weights)
```

```python
import functools

import jax
import jax.numpy as jnp
from jax import lax
from jax.experimental import pallas as pl
from jax.experimental.pallas import tpu as pltpu
from jax.sharding import PartitionSpec as P

LANES = 128
VMEM = pl.BlockSpec(memory_space=pltpu.VMEM)
SMEM = pl.BlockSpec(memory_space=pltpu.SMEM)
BIG = pltpu.CompilerParams(vmem_limit_bytes=48 << 20)


def split_kernel(n, chunks, grads_ref, *rest):
    outs, wide = rest[:n], rest[n]
    me = lax.axis_index("shard")
    wide[...] = grads_ref[...].astype(jnp.float32).reshape(wide.shape)
    for k in range(n):
        row = me ^ k
        first = (row // 8) * (chunks * 8) + row % 8
        outs[k][...] = wide[pl.ds(first, chunks, stride=8), :].astype(jnp.bfloat16)


def join_kernel(n, chunks, *rest):
    ins, out_ref, wide = rest[:n], rest[n], rest[n + 1]
    me = lax.axis_index("shard")
    for k in range(n):
        row = me ^ k
        first = (row // 8) * (chunks * 8) + row % 8
        wide[pl.ds(first, chunks, stride=8), :] = ins[k][...].astype(jnp.float32)
    out_ref[...] = wide[...].reshape(out_ref.shape).astype(jnp.bfloat16)


def segment_rows(squares, table, bounds):
    tile = lax.broadcasted_iota(jnp.int32, (8, LANES), 0) * LANES
    tile = tile + lax.broadcasted_iota(jnp.int32, (8, LANES), 1)
    table[...] = jnp.zeros_like(table)
    count = bounds.shape[0] - 3

    def segment(k, carry):
        low, high = bounds[k], bounds[k + 1]

        def step(t, total):
            place = tile + t * (8 * LANES)
            piece = squares[pl.ds(pl.multiple_of(t * 8, 8), 8), :]
            return total + jnp.where((place >= low) & (place < high), piece, 0.0)

        total = lax.fori_loop(
            low // (8 * LANES),
            (high + (8 * LANES - 1)) // (8 * LANES),
            step,
            jnp.zeros((8, LANES), jnp.float32),
        )
        table[pl.ds(k, 1), :] = jnp.sum(total, axis=0, keepdims=True)
        return carry

    lax.fori_loop(bounds[count + 1], bounds[count + 2], segment, 0)


def weights_kernel(lengths_ref, weights_ref, sums_ref, bounds_ref, squares, table):
    chunks = weights_ref.shape[0]
    width = chunks * LANES
    count = lengths_ref.shape[0]
    index = lax.axis_index("shard") * lax.axis_size("tensor") + lax.axis_index("tensor")
    base = index * width

    def walk(k, carry):
        at, first, last = carry
        bounds_ref[k] = jnp.clip(at, 0, width)
        then = at + lengths_ref[k]
        first = jnp.where(then <= 0, k + 1, first)
        last = jnp.where(at < width, k + 1, last)
        return (then, first, last)

    at, first, last = lax.fori_loop(
        0, count, walk, (-base, jnp.int32(0), jnp.int32(0))
    )
    bounds_ref[count] = jnp.clip(at, 0, width)
    bounds_ref[count + 1] = first
    bounds_ref[count + 2] = last
    squares[...] = weights_ref[...] * weights_ref[...]
    segment_rows(squares, table, bounds_ref)
    sums_ref[...] = jnp.sum(table[...].T, axis=0, keepdims=True)


def update_kernel(n, step_ref, bounds_ref, sums_ref, weights_ref, moment1_ref, moment2_ref, *rest):
    pieces = rest[:n]
    new1_ref, new2_ref, update_ref, send_ref = rest[n : n + 4]
    squares, table = rest[n + 4 :]

    def power(base):
        return lax.fori_loop(
            0, step_ref[0], lambda i, p: p * base, jnp.full((8, LANES), 1.0, jnp.float32)
        )

    scale1 = (1.0 / (1.0 - power(jnp.float32(0.9))))[0:1, :]
    scale2 = (1.0 / (1.0 - power(jnp.float32(0.999))))[0:1, :]
    grad = pieces[0][...].astype(jnp.float32)
    for piece in pieces[1:]:
        grad = grad + piece[...].astype(jnp.float32)
    new1 = 0.9 * moment1_ref[...] + 0.1 * grad
    new2 = 0.999 * moment2_ref[...] + 0.001 * grad * grad
    new1_ref[...] = new1
    new2_ref[...] = new2
    update = (new1 * scale1) / (jnp.sqrt(new2 * scale2) + 1e-06) + 0.1 * weights_ref[...]
    update_ref[...] = update
    squares[...] = update * update
    segment_rows(squares, table, bounds_ref)
    mine = jnp.sum(table[...].T, axis=0, keepdims=True)
    which = lax.broadcasted_iota(jnp.int32, (8, LANES), 0)
    both = jnp.where(which == 0, sums_ref[...], jnp.where(which == 1, mine, 0.0))
    send_ref[...] = jnp.broadcast_to(both[None], send_ref.shape)


def weights_out_kernel(
    bounds_ref, sums_ref, weights_ref, update_ref, new_ref, narrow_ref, table, spread
):
    chunks = weights_ref.shape[0]
    count = bounds_ref.shape[0] - 3
    both = jnp.sum(sums_ref[...], axis=0)
    ratio = 0.25 * (jnp.sqrt(both[0:1, :]) / jnp.maximum(jnp.sqrt(both[1:2, :]), 1.0))
    table[...] = jnp.broadcast_to(ratio, (LANES, LANES)).T
    place = lax.broadcasted_iota(jnp.int32, (chunks, LANES), 0) * LANES
    place = place + lax.broadcasted_iota(jnp.int32, (chunks, LANES), 1)
    first = bounds_ref[count + 1]
    spread[...] = jnp.broadcast_to(table[pl.ds(first, 1), :], spread.shape)

    def segment(k, carry):
        spread[...] = jnp.where(place >= bounds_ref[k], table[pl.ds(k, 1), :], spread[...])
        return carry

    lax.fori_loop(first + 1, bounds_ref[count + 2], segment, 0)
    new = weights_ref[...] - spread[...] * update_ref[...]
    new_ref[...] = new
    narrow_ref[...] = new.astype(jnp.bfloat16)


def swap(value, axis, size, k):
    return lax.ppermute(value, axis, [(i, i ^ k) for i in range(size)])


def local(step, lengths, grads, weights, moment1, moment2):
    n = lax.axis_size("shard")
    everyone = n * lax.axis_size("tensor")
    width = weights.shape[0]
    chunks = width // LANES
    count = lengths.shape[0]
    flat = lambda dtype: jax.ShapeDtypeStruct((chunks, LANES), dtype)
    rows = grads.reshape(n // 8, 8, chunks, LANES).transpose(0, 2, 1, 3)
    pieces = pl.pallas_call(
        functools.partial(split_kernel, n, chunks),
        out_shape=[flat(jnp.bfloat16)] * n,
        in_specs=[VMEM],
        out_specs=[VMEM] * n,
        scratch_shapes=[pltpu.VMEM((n * chunks, LANES), jnp.float32)],
        compiler_params=BIG,
        name="split",
    )(rows)
    pieces = [pieces[0]] + [swap(pieces[k], "shard", n, k) for k in range(1, n)]
    weights = weights.reshape(chunks, LANES)
    moment1 = moment1.reshape(chunks, LANES)
    moment2 = moment2.reshape(chunks, LANES)
    square_table = [
        pltpu.VMEM((chunks, LANES), jnp.float32),
        pltpu.VMEM((LANES, LANES), jnp.float32),
    ]
    sums, bounds = pl.pallas_call(
        weights_kernel,
        out_shape=[
            jax.ShapeDtypeStruct((1, LANES), jnp.float32),
            jax.ShapeDtypeStruct((count + 3,), jnp.int32),
        ],
        in_specs=[SMEM, VMEM],
        out_specs=[VMEM, SMEM],
        scratch_shapes=square_table,
        compiler_params=BIG,
        cost_estimate=pl.CostEstimate(flops=8 * width, bytes_accessed=4 * width, transcendentals=0),
        name="weight_squares",
    )(lengths, weights)
    new1, new2, update, send = pl.pallas_call(
        functools.partial(update_kernel, n),
        out_shape=[flat(jnp.float32)] * 3
        + [jax.ShapeDtypeStruct((everyone, 8, LANES), jnp.float32)],
        in_specs=[SMEM, SMEM] + [VMEM] * (4 + n),
        out_specs=[VMEM] * 4,
        scratch_shapes=square_table,
        compiler_params=BIG,
        name="update",
    )(step, bounds, sums, weights, moment1, moment2, *pieces)
    sums = lax.all_to_all(send, ("shard", "tensor"), 0, 0, tiled=True)
    new, narrow = pl.pallas_call(
        weights_out_kernel,
        out_shape=[flat(jnp.float32), flat(jnp.bfloat16)],
        in_specs=[SMEM, VMEM, VMEM, VMEM],
        out_specs=[VMEM] * 2,
        scratch_shapes=[
            pltpu.VMEM((LANES, LANES), jnp.float32),
            pltpu.VMEM((chunks, LANES), jnp.float32),
        ],
        compiler_params=BIG,
        name="new_weights",
    )(bounds, sums, weights, update)
    gathered = {0: narrow}
    for k in range(2, n, 2):
        gathered[k] = swap(narrow, "shard", n, k)
    for k in range(0, n, 2):
        gathered[k + 1] = swap(gathered[k], "shard", n, 1)
    joined = pl.pallas_call(
        functools.partial(join_kernel, n, chunks),
        out_shape=jax.ShapeDtypeStruct((n // 8, chunks, 8, LANES), jnp.bfloat16),
        in_specs=[VMEM] * n,
        out_specs=VMEM,
        scratch_shapes=[pltpu.VMEM((n * chunks, LANES), jnp.float32)],
        compiler_params=BIG,
        name="join",
    )(*[gathered[k] for k in range(n)])
    train = joined.transpose(0, 2, 1, 3).reshape(n, 1, width)
    return (new.reshape(width), new1.reshape(width), new2.reshape(width), train)


def solution(mesh):
    whole = P(("shard", "tensor"))
    return jax.shard_map(
        local,
        mesh=mesh,
        in_specs=(P(), P(), P("shard", None, "tensor", None), whole, whole, whole),
        out_specs=(whole, whole, whole, P(None, "tensor", None)),
        check_vma=False,
    )
```

```python
import functools
import math

import jax
import jax.numpy as jnp
from jax import lax
from jax.experimental import pallas as pl
from jax.experimental.pallas import tpu as pltpu
from jax.sharding import PartitionSpec as P

LANES = 128
TILE = 64
PARTS = 4
VMEM = pl.BlockSpec(memory_space=pltpu.VMEM)
SMEM = pl.BlockSpec(memory_space=pltpu.SMEM)
HBM = pl.BlockSpec(memory_space=pltpu.HBM)
BIG = pltpu.CompilerParams(vmem_limit_bytes=48 << 20)


def split_kernel(n, chunks, grads_ref, *rest):
    outs, (held, wide, sems) = rest[:n], rest[n:]
    me = lax.axis_index("shard")
    parts, depth = held.shape[0], held.shape[2]
    copies = []
    for part in range(parts):
        source = grads_ref.at[:, pl.ds(part * depth, depth)]
        copies.append(pltpu.make_async_copy(source, held.at[part], sems.at[part]))
        copies[-1].start()
    for part in range(parts):
        copies[part].wait()
        wide[part] = held[part].astype(jnp.float32).reshape(wide.shape[1:])
        for k in range(n):
            row = me ^ k
            first = (row // 8) * (depth * 8) + row % 8
            taken = wide[part, pl.ds(first, depth, stride=8), :]
            outs[k][part * depth : (part + 1) * depth, :] = taken.astype(jnp.bfloat16)


def join_kernel(n, chunks, *rest):
    ins, out_ref, (held, wide, sems) = rest[:n], rest[n], rest[n + 1 :]
    me = lax.axis_index("shard")
    parts, depth = held.shape[0], held.shape[2]
    copies = []
    for part in range(parts):
        for k in range(n):
            row = me ^ k
            first = (row // 8) * (depth * 8) + row % 8
            taken = ins[k][part * depth : (part + 1) * depth, :]
            wide[part, pl.ds(first, depth, stride=8), :] = taken.astype(jnp.float32)
        held[part] = wide[part].reshape(held.shape[1:]).astype(jnp.bfloat16)
        target = out_ref.at[:, pl.ds(part * depth, depth)]
        copies.append(pltpu.make_async_copy(held.at[part], target, sems.at[part]))
        copies[-1].start()
    for copy in copies:
        copy.wait()


def store_kernel(new1_ref, new2_ref, new_ref, out1_ref, out2_ref, out_ref, sems):
    pairs = ((new1_ref, out1_ref), (new2_ref, out2_ref), (new_ref, out_ref))
    copies = [pltpu.make_async_copy(*pair, sems.at[i]) for i, pair in enumerate(pairs)]
    for copy in copies:
        copy.start()
    for copy in copies:
        copy.wait()


def places(rows):
    place = lax.broadcasted_iota(jnp.int32, (rows, LANES), 0) * LANES
    return place + lax.broadcasted_iota(jnp.int32, (rows, LANES), 1)


def segment_rows(squares, table, bounds):
    rows = math.gcd(squares.shape[0], TILE)
    size = rows * LANES
    place = places(rows)
    table[...] = jnp.zeros_like(table)
    count = bounds.shape[0] - 3

    def segment(k, carry):
        low, high = bounds[k], bounds[k + 1]

        def step(t, total):
            piece = squares[pl.ds(pl.multiple_of(t * rows, rows), rows), :]
            at = t * size
            inside = (place >= low - at) & (place < high - at)
            return total + jnp.where(inside, piece, 0.0)

        total = lax.fori_loop(
            low // size,
            (high + (size - 1)) // size,
            step,
            jnp.zeros((rows, LANES), jnp.float32),
        )
        table[pl.ds(k, 1), :] = jnp.sum(total, axis=0, keepdims=True)
        return carry

    lax.fori_loop(bounds[count + 1], bounds[count + 2], segment, 0)


def weights_kernel(lengths_ref, weights_ref, sums_ref, bounds_ref, squares, table):
    chunks = weights_ref.shape[0]
    width = chunks * LANES
    count = lengths_ref.shape[0]
    index = lax.axis_index("shard") * lax.axis_size("tensor") + lax.axis_index("tensor")
    base = index * width

    def walk(k, carry):
        at, first, last = carry
        bounds_ref[k] = jnp.clip(at, 0, width)
        then = at + lengths_ref[k]
        first = jnp.where(then <= 0, k + 1, first)
        last = jnp.where(at < width, k + 1, last)
        return (then, first, last)

    at, first, last = lax.fori_loop(
        0, count, walk, (-base, jnp.int32(0), jnp.int32(0))
    )
    bounds_ref[count] = jnp.clip(at, 0, width)
    bounds_ref[count + 1] = first
    bounds_ref[count + 2] = last
    squares[...] = weights_ref[...] * weights_ref[...]
    segment_rows(squares, table, bounds_ref)
    sums_ref[...] = jnp.sum(table[...].T, axis=0, keepdims=True)


def update_kernel(n, step_ref, bounds_ref, sums_ref, weights_ref, moment1_ref, moment2_ref, *rest):
    pieces = rest[:n]
    new1_ref, new2_ref, update_ref, send_ref = rest[n : n + 4]
    squares, table = rest[n + 4 :]

    def power(base):
        return lax.fori_loop(
            0, step_ref[0], lambda i, p: p * base, jnp.full((8, LANES), 1.0, jnp.float32)
        )

    scale1 = (1.0 / (1.0 - power(jnp.float32(0.9))))[0:1, :]
    scale2 = (1.0 / (1.0 - power(jnp.float32(0.999))))[0:1, :]
    chunks = weights_ref.shape[0]
    rows = math.gcd(chunks, TILE)

    def block(t, carry):
        part = pl.ds(pl.multiple_of(t * rows, rows), rows)
        grad = pieces[0][part, :].astype(jnp.float32)
        for piece in pieces[1:]:
            grad = grad + piece[part, :].astype(jnp.float32)
        new1 = 0.9 * moment1_ref[part, :] + 0.1 * grad
        new2 = 0.999 * moment2_ref[part, :] + 0.001 * grad * grad
        new1_ref[part, :] = new1
        new2_ref[part, :] = new2
        update = (new1 * scale1) / (jnp.sqrt(new2 * scale2) + 1e-06)
        update = update + 0.1 * weights_ref[part, :]
        update_ref[part, :] = update
        squares[part, :] = update * update
        return carry

    lax.fori_loop(0, chunks // rows, block, 0, unroll=2)
    segment_rows(squares, table, bounds_ref)
    mine = jnp.sum(table[...].T, axis=0, keepdims=True)
    which = lax.broadcasted_iota(jnp.int32, (2, LANES), 0)
    both = jnp.where(which == 0, sums_ref[...], mine)
    send_ref[...] = jnp.broadcast_to(both[None], send_ref.shape)


def weights_out_kernel(
    bounds_ref, sums_ref, weights_ref, update_ref, new_ref, narrow_ref, table
):
    chunks = weights_ref.shape[0]
    rows = math.gcd(chunks, TILE)
    size = rows * LANES
    place = places(rows)
    count = bounds_ref.shape[0] - 3
    both = jnp.sum(sums_ref[...], axis=0)
    ratio = 0.25 * (jnp.sqrt(both[0:1, :]) / jnp.maximum(jnp.sqrt(both[1:2, :]), 1.0))
    table[...] = jnp.broadcast_to(ratio, (LANES, LANES)).T

    def segment(k, carry):
        low, high = bounds_ref[k], bounds_ref[k + 1]
        scale = table[pl.ds(k, 1), :]

        def step(t, carry):
            part = pl.ds(pl.multiple_of(t * rows, rows), rows)
            new = weights_ref[part, :] - scale * update_ref[part, :]
            new = jnp.where(place >= low - t * size, new, new_ref[part, :])
            new_ref[part, :] = new
            narrow_ref[part, :] = new.astype(jnp.bfloat16)
            return carry

        return lax.fori_loop(low // size, (high + (size - 1)) // size, step, carry)

    lax.fori_loop(bounds_ref[count + 1], bounds_ref[count + 2], segment, 0)


def swap(value, axis, size, k):
    return lax.ppermute(value, axis, [(i, i ^ k) for i in range(size)])


def local(step, lengths, grads, weights, moment1, moment2):
    n = lax.axis_size("shard")
    everyone = n * lax.axis_size("tensor")
    width = weights.shape[0]
    chunks = width // LANES
    count = lengths.shape[0]
    flat = lambda dtype: jax.ShapeDtypeStruct((chunks, LANES), dtype)
    rows = grads.reshape(n // 8, 8, chunks, LANES).transpose(0, 2, 1, 3)
    parts = math.gcd(PARTS, chunks // 16)
    depth = chunks // parts
    staging = [
        pltpu.VMEM((parts, n // 8, depth, 8, LANES), jnp.bfloat16),
        pltpu.VMEM((parts, n * depth, LANES), jnp.float32),
        pltpu.SemaphoreType.DMA((parts,)),
    ]
    pieces = pl.pallas_call(
        functools.partial(split_kernel, n, chunks),
        out_shape=[flat(jnp.bfloat16)] * n,
        in_specs=[HBM],
        out_specs=[VMEM] * n,
        scratch_shapes=staging,
        compiler_params=BIG,
        name="split",
    )(pltpu.with_memory_space_constraint(rows, pltpu.HBM))
    pieces = [pieces[0]] + [swap(pieces[k], "shard", n, k) for k in range(1, n)]
    weights = weights.reshape(chunks, LANES)
    moment1 = moment1.reshape(chunks, LANES)
    moment2 = moment2.reshape(chunks, LANES)
    square_table = [
        pltpu.VMEM((chunks, LANES), jnp.float32),
        pltpu.VMEM((LANES, LANES), jnp.float32),
    ]
    sums, bounds = pl.pallas_call(
        weights_kernel,
        out_shape=[
            jax.ShapeDtypeStruct((1, LANES), jnp.float32),
            jax.ShapeDtypeStruct((count + 3,), jnp.int32),
        ],
        in_specs=[SMEM, VMEM],
        out_specs=[VMEM, SMEM],
        scratch_shapes=square_table,
        compiler_params=BIG,
        cost_estimate=pl.CostEstimate(flops=8 * width, bytes_accessed=4 * width, transcendentals=0),
        name="weight_squares",
    )(lengths, weights)
    new1, new2, update, send = pl.pallas_call(
        functools.partial(update_kernel, n),
        out_shape=[flat(jnp.float32)] * 3
        + [jax.ShapeDtypeStruct((everyone, 2, LANES), jnp.float32)],
        in_specs=[SMEM, SMEM] + [VMEM] * (4 + n),
        out_specs=[VMEM] * 4,
        scratch_shapes=square_table,
        compiler_params=BIG,
        name="update",
    )(step, bounds, sums, weights, moment1, moment2, *pieces)
    sums = lax.all_to_all(send, ("shard", "tensor"), 0, 0, tiled=True)
    new, narrow = pl.pallas_call(
        weights_out_kernel,
        out_shape=[flat(jnp.float32), flat(jnp.bfloat16)],
        in_specs=[SMEM, VMEM, VMEM, VMEM],
        out_specs=[VMEM] * 2,
        scratch_shapes=[pltpu.VMEM((LANES, LANES), jnp.float32)],
        compiler_params=BIG,
        name="new_weights",
    )(bounds, sums, weights, update)
    gathered = {0: narrow}
    for k in range(2, n, 2):
        gathered[k] = swap(narrow, "shard", n, k)
    for k in range(0, n, 2):
        gathered[k + 1] = swap(gathered[k], "shard", n, 1)
    new1, new2, new = pl.pallas_call(
        store_kernel,
        out_shape=[flat(jnp.float32)] * 3,
        in_specs=[VMEM] * 3,
        out_specs=[HBM] * 3,
        scratch_shapes=[pltpu.SemaphoreType.DMA((3,))],
        compiler_params=BIG,
        cost_estimate=pl.CostEstimate(flops=0, bytes_accessed=12 * width, transcendentals=0),
        name="store",
    )(new1, new2, new)
    joined = pl.pallas_call(
        functools.partial(join_kernel, n, chunks),
        out_shape=jax.ShapeDtypeStruct((n // 8, chunks, 8, LANES), jnp.bfloat16),
        in_specs=[VMEM] * n,
        out_specs=HBM,
        scratch_shapes=staging,
        compiler_params=BIG,
        name="join",
    )(*[gathered[k] for k in range(n)])
    train = joined.transpose(0, 2, 1, 3).reshape(n, 1, width)
    return (new.reshape(width), new1.reshape(width), new2.reshape(width), train)


def solution(mesh):
    whole = P(("shard", "tensor"))
    return jax.shard_map(
        local,
        mesh=mesh,
        in_specs=(P(), P(), P("shard", None, "tensor", None), whole, whole, whole),
        out_specs=(whole, whole, whole, P(None, "tensor", None)),
        check_vma=False,
    )
```

```python
import functools
import math

import jax
import jax.numpy as jnp
from jax import lax
from jax.experimental import pallas as pl
from jax.experimental.pallas import tpu as pltpu
from jax.sharding import PartitionSpec as P

LANES = 128
TILE = 64
PARTS = 4
ORDER = (2, 4, 3, 5, 6, 7, 1)
EARLY = 3
VMEM = pl.BlockSpec(memory_space=pltpu.VMEM)
SMEM = pl.BlockSpec(memory_space=pltpu.SMEM)
HBM = pl.BlockSpec(memory_space=pltpu.HBM)
BIG = pltpu.CompilerParams(vmem_limit_bytes=48 << 20)


def split_kernel(n, chunks, grads_ref, *rest):
    outs, (held, wide, sems) = rest[:n], rest[n:]
    me = lax.axis_index("shard")
    parts, depth = held.shape[0], held.shape[2]
    copies = []
    for part in range(parts):
        source = grads_ref.at[:, pl.ds(part * depth, depth)]
        copies.append(pltpu.make_async_copy(source, held.at[part], sems.at[part]))
        copies[-1].start()
    for part in range(parts):
        copies[part].wait()
        wide[part] = held[part].astype(jnp.float32).reshape(wide.shape[1:])
        for k in range(n):
            row = me ^ k
            first = (row // 8) * (depth * 8) + row % 8
            taken = wide[part, pl.ds(first, depth, stride=8), :]
            outs[k][part * depth : (part + 1) * depth, :] = taken.astype(jnp.bfloat16)


def join_kernel(n, chunks, *rest):
    ins, out_ref, (held, wide, sems) = rest[:n], rest[n], rest[n + 1 :]
    me = lax.axis_index("shard")
    parts, depth = held.shape[0], held.shape[2]
    copies = []
    for part in range(parts):
        for k in range(n):
            row = me ^ k
            first = (row // 8) * (depth * 8) + row % 8
            taken = ins[k][part * depth : (part + 1) * depth, :]
            wide[part, pl.ds(first, depth, stride=8), :] = taken.astype(jnp.float32)
        held[part] = wide[part].reshape(held.shape[1:]).astype(jnp.bfloat16)
        target = out_ref.at[:, pl.ds(part * depth, depth)]
        copies.append(pltpu.make_async_copy(held.at[part], target, sems.at[part]))
        copies[-1].start()
    for copy in copies:
        copy.wait()


def store_kernel(new1_ref, new2_ref, new_ref, out1_ref, out2_ref, out_ref, sems):
    pairs = ((new1_ref, out1_ref), (new2_ref, out2_ref), (new_ref, out_ref))
    copies = [pltpu.make_async_copy(*pair, sems.at[i]) for i, pair in enumerate(pairs)]
    for copy in copies:
        copy.start()
    for copy in copies:
        copy.wait()


def places(rows):
    place = lax.broadcasted_iota(jnp.int32, (rows, LANES), 0) * LANES
    return place + lax.broadcasted_iota(jnp.int32, (rows, LANES), 1)


def total_of(pieces, part):
    total = pieces[0][part, :].astype(jnp.float32)
    for piece in pieces[1:]:
        total = total + piece[part, :].astype(jnp.float32)
    return total


def segment_rows(squares, table, bounds):
    rows = math.gcd(squares.shape[0], TILE)
    size = rows * LANES
    place = places(rows)
    table[...] = jnp.zeros_like(table)
    count = bounds.shape[0] - 3

    def segment(k, carry):
        low, high = bounds[k], bounds[k + 1]

        def step(t, total):
            piece = squares[pl.ds(pl.multiple_of(t * rows, rows), rows), :]
            at = t * size
            inside = (place >= low - at) & (place < high - at)
            return total + jnp.where(inside, piece, 0.0)

        total = lax.fori_loop(
            low // size,
            (high + (size - 1)) // size,
            step,
            jnp.zeros((rows, LANES), jnp.float32),
        )
        table[pl.ds(k, 1), :] = jnp.sum(total, axis=0, keepdims=True)
        return carry

    lax.fori_loop(bounds[count + 1], bounds[count + 2], segment, 0)


def early_kernel(n, lengths_ref, weights_hbm, moment1_hbm, moment2_hbm, *rest):
    pieces = rest[:n]
    weights_ref, moment1_ref, moment2_ref, partial_ref, sums_ref, bounds_ref = rest[n : n + 6]
    squares, table, sems = rest[n + 6 :]
    chunks = weights_ref.shape[0]
    pairs = ((weights_hbm, weights_ref), (moment1_hbm, moment1_ref), (moment2_hbm, moment2_ref))
    copies = [pltpu.make_async_copy(*pair, sems.at[i]) for i, pair in enumerate(pairs)]
    for copy in copies:
        copy.start()
    width = chunks * LANES
    count = lengths_ref.shape[0]
    index = lax.axis_index("shard") * lax.axis_size("tensor") + lax.axis_index("tensor")
    base = index * width

    def walk(k, carry):
        at, first, last = carry
        bounds_ref[k] = jnp.clip(at, 0, width)
        then = at + lengths_ref[k]
        first = jnp.where(then <= 0, k + 1, first)
        last = jnp.where(at < width, k + 1, last)
        return (then, first, last)

    at, first, last = lax.fori_loop(
        0, count, walk, (-base, jnp.int32(0), jnp.int32(0))
    )
    bounds_ref[count] = jnp.clip(at, 0, width)
    bounds_ref[count + 1] = first
    bounds_ref[count + 2] = last
    rows = math.gcd(chunks, TILE)

    def add(t, carry):
        part = pl.ds(pl.multiple_of(t * rows, rows), rows)
        partial_ref[part, :] = total_of(pieces, part)
        return carry

    lax.fori_loop(0, chunks // rows, add, 0)
    for copy in copies:
        copy.wait()
    squares[...] = weights_ref[...] * weights_ref[...]
    segment_rows(squares, table, bounds_ref)
    sums_ref[...] = jnp.sum(table[...].T, axis=0, keepdims=True)


def update_kernel(n, step_ref, bounds_ref, sums_ref, weights_ref, moment1_ref, moment2_ref, *rest):
    partial_ref, pieces = rest[0], rest[1 : n + 1]
    rest = rest[1:]
    new1_ref, new2_ref, update_ref, send_ref = rest[n : n + 4]
    squares, table = rest[n + 4 :]

    def power(base):
        return lax.fori_loop(
            0, step_ref[0], lambda i, p: p * base, jnp.full((8, LANES), 1.0, jnp.float32)
        )

    scale1 = (1.0 / (1.0 - power(jnp.float32(0.9))))[0:1, :]
    scale2 = (1.0 / (1.0 - power(jnp.float32(0.999))))[0:1, :]
    chunks = weights_ref.shape[0]
    rows = math.gcd(chunks, TILE)

    def block(t, carry):
        part = pl.ds(pl.multiple_of(t * rows, rows), rows)
        grad = partial_ref[part, :] + total_of(pieces, part)
        new1 = 0.9 * moment1_ref[part, :] + 0.1 * grad
        new2 = 0.999 * moment2_ref[part, :] + 0.001 * grad * grad
        new1_ref[part, :] = new1
        new2_ref[part, :] = new2
        update = (new1 * scale1) / (jnp.sqrt(new2 * scale2) + 1e-06)
        update = update + 0.1 * weights_ref[part, :]
        update_ref[part, :] = update
        squares[part, :] = update * update
        return carry

    lax.fori_loop(0, chunks // rows, block, 0, unroll=2)
    segment_rows(squares, table, bounds_ref)
    mine = jnp.sum(table[...].T, axis=0, keepdims=True)
    which = lax.broadcasted_iota(jnp.int32, (2, LANES), 0)
    both = jnp.where(which == 0, sums_ref[...], mine)
    send_ref[...] = jnp.broadcast_to(both[None], send_ref.shape)


def weights_out_kernel(
    bounds_ref, sums_ref, weights_ref, update_ref, new_ref, narrow_ref, table
):
    chunks = weights_ref.shape[0]
    rows = math.gcd(chunks, TILE)
    size = rows * LANES
    place = places(rows)
    count = bounds_ref.shape[0] - 3
    both = jnp.sum(sums_ref[...], axis=0)
    ratio = 0.25 * (jnp.sqrt(both[0:1, :]) / jnp.maximum(jnp.sqrt(both[1:2, :]), 1.0))
    table[...] = jnp.broadcast_to(ratio, (LANES, LANES)).T

    def segment(k, carry):
        low, high = bounds_ref[k], bounds_ref[k + 1]
        scale = table[pl.ds(k, 1), :]

        def step(t, carry):
            part = pl.ds(pl.multiple_of(t * rows, rows), rows)
            new = weights_ref[part, :] - scale * update_ref[part, :]
            new = jnp.where(place >= low - t * size, new, new_ref[part, :])
            new_ref[part, :] = new
            narrow_ref[part, :] = new.astype(jnp.bfloat16)
            return carry

        return lax.fori_loop(low // size, (high + (size - 1)) // size, step, carry)

    lax.fori_loop(bounds_ref[count + 1], bounds_ref[count + 2], segment, 0)


def exchange_order(n):
    first = [k for k in ORDER if k < n]
    return first + [k for k in range(1, n) if k not in first]


def swap(value, axis, size, k):
    return lax.ppermute(value, axis, [(i, i ^ k) for i in range(size)])


def local(step, lengths, grads, weights, moment1, moment2):
    n = lax.axis_size("shard")
    everyone = n * lax.axis_size("tensor")
    width = weights.shape[0]
    chunks = width // LANES
    count = lengths.shape[0]
    flat = lambda dtype: jax.ShapeDtypeStruct((chunks, LANES), dtype)
    rows = grads.reshape(n // 8, 8, chunks, LANES).transpose(0, 2, 1, 3)
    parts = math.gcd(PARTS, chunks // 16)
    depth = chunks // parts
    staging = [
        pltpu.VMEM((parts, n // 8, depth, 8, LANES), jnp.bfloat16),
        pltpu.VMEM((parts, n * depth, LANES), jnp.float32),
        pltpu.SemaphoreType.DMA((parts,)),
    ]
    pieces = pl.pallas_call(
        functools.partial(split_kernel, n, chunks),
        out_shape=[flat(jnp.bfloat16)] * n,
        in_specs=[HBM],
        out_specs=[VMEM] * n,
        scratch_shapes=staging,
        compiler_params=BIG,
        name="split",
    )(pltpu.with_memory_space_constraint(rows, pltpu.HBM))
    order = exchange_order(n)
    pieces = [pieces[0]] + [swap(pieces[k], "shard", n, k) for k in order]
    early, late = pieces[: EARLY + 1], pieces[EARLY + 1 :]
    square_table = [
        pltpu.VMEM((chunks, LANES), jnp.float32),
        pltpu.VMEM((LANES, LANES), jnp.float32),
    ]
    stored = [
        pltpu.with_memory_space_constraint(value.reshape(chunks, LANES), pltpu.HBM)
        for value in (weights, moment1, moment2)
    ]
    weights, moment1, moment2, partial, sums, bounds = pl.pallas_call(
        functools.partial(early_kernel, len(early)),
        out_shape=[flat(jnp.float32)] * 4
        + [
            jax.ShapeDtypeStruct((1, LANES), jnp.float32),
            jax.ShapeDtypeStruct((count + 3,), jnp.int32),
        ],
        in_specs=[SMEM] + [HBM] * 3 + [VMEM] * len(early),
        out_specs=[VMEM] * 5 + [SMEM],
        scratch_shapes=square_table + [pltpu.SemaphoreType.DMA((3,))],
        compiler_params=BIG,
        cost_estimate=pl.CostEstimate(
            flops=8 * width, bytes_accessed=24 * width, transcendentals=0
        ),
        name="early",
    )(lengths, *stored, *early)
    new1, new2, update, send = pl.pallas_call(
        functools.partial(update_kernel, len(late)),
        out_shape=[flat(jnp.float32)] * 3
        + [jax.ShapeDtypeStruct((everyone, 2, LANES), jnp.float32)],
        in_specs=[SMEM, SMEM] + [VMEM] * (5 + len(late)),
        out_specs=[VMEM] * 4,
        scratch_shapes=square_table,
        compiler_params=BIG,
        name="update",
    )(step, bounds, sums, weights, moment1, moment2, partial, *late)
    sums = lax.all_to_all(send, ("shard", "tensor"), 0, 0, tiled=True)
    new, narrow = pl.pallas_call(
        weights_out_kernel,
        out_shape=[flat(jnp.float32), flat(jnp.bfloat16)],
        in_specs=[SMEM, VMEM, VMEM, VMEM],
        out_specs=[VMEM] * 2,
        scratch_shapes=[pltpu.VMEM((LANES, LANES), jnp.float32)],
        compiler_params=BIG,
        name="new_weights",
    )(bounds, sums, weights, update)
    gathered = {0: narrow}
    for k in range(2, n, 2):
        gathered[k] = swap(narrow, "shard", n, k)
    new1, new2, new = pl.pallas_call(
        store_kernel,
        out_shape=[flat(jnp.float32)] * 3,
        in_specs=[VMEM] * 3,
        out_specs=[HBM] * 3,
        scratch_shapes=[pltpu.SemaphoreType.DMA((3,))],
        compiler_params=BIG,
        cost_estimate=pl.CostEstimate(flops=0, bytes_accessed=12 * width, transcendentals=0),
        name="store",
    )(new1, new2, new)
    for k in range(0, n, 2):
        gathered[k + 1] = swap(gathered[k], "shard", n, 1)
    joined = pl.pallas_call(
        functools.partial(join_kernel, n, chunks),
        out_shape=jax.ShapeDtypeStruct((n // 8, chunks, 8, LANES), jnp.bfloat16),
        in_specs=[VMEM] * n,
        out_specs=HBM,
        scratch_shapes=staging,
        compiler_params=BIG,
        name="join",
    )(*[gathered[k] for k in range(n)])
    train = joined.transpose(0, 2, 1, 3).reshape(n, 1, width)
    return (new.reshape(width), new1.reshape(width), new2.reshape(width), train)


def solution(mesh):
    whole = P(("shard", "tensor"))
    return jax.shard_map(
        local,
        mesh=mesh,
        in_specs=(P(), P(), P("shard", None, "tensor", None), whole, whole, whole),
        out_specs=(whole, whole, whole, P(None, "tensor", None)),
        check_vma=False,
    )
```

```python
import functools
import math

import jax
import jax.numpy as jnp
from jax import lax
from jax.experimental import pallas as pl
from jax.experimental.pallas import tpu as pltpu
from jax.sharding import PartitionSpec as P

LANES = 128
TILE = 64
PARTS = 4
ORDER = (2, 4, 3, 5, 6, 7, 1)
EARLY = 3
VMEM = pl.BlockSpec(memory_space=pltpu.VMEM)
SMEM = pl.BlockSpec(memory_space=pltpu.SMEM)
HBM = pl.BlockSpec(memory_space=pltpu.HBM)
BIG = pltpu.CompilerParams(vmem_limit_bytes=48 << 20)


def split_kernel(n, chunks, grads_ref, *rest):
    outs, (held, wide, sems) = rest[:n], rest[n:]
    me = lax.axis_index("shard")
    parts, depth = held.shape[0], held.shape[2]
    copies = []
    for part in range(parts):
        source = grads_ref.at[:, pl.ds(part * depth, depth)]
        copies.append(pltpu.make_async_copy(source, held.at[part], sems.at[part]))
        copies[-1].start()
    for part in range(parts):
        copies[part].wait()
        wide[part] = held[part].astype(jnp.float32).reshape(wide.shape[1:])
        for k in range(n):
            row = me ^ k
            first = (row // 8) * (depth * 8) + row % 8
            taken = wide[part, pl.ds(first, depth, stride=8), :]
            outs[k][part * depth : (part + 1) * depth, :] = taken.astype(jnp.bfloat16)


def lay(rows, wide, part, depth, ins):
    me = lax.axis_index("shard")
    for k, value in zip(rows, ins):
        row = me ^ k
        first = (row // 8) * (depth * 8) + row % 8
        taken = value[part * depth : (part + 1) * depth, :]
        wide[part, pl.ds(first, depth, stride=8), :] = taken.astype(jnp.float32)


def lay_kernel(rows, *rest):
    ins, wide = rest[:-1], rest[-1]
    parts = wide.shape[0]
    for part in range(parts):
        lay(rows, wide, part, ins[0].shape[0] // parts, ins)


def join_kernel(rows, *rest):
    ins, (out_ref, wide, held, sems) = rest[1:-4], rest[-4:]
    parts, depth = held.shape[0], held.shape[2]
    copies = []
    for part in range(parts):
        lay(rows, wide, part, depth, ins)
        held[part] = wide[part].reshape(held.shape[1:]).astype(jnp.bfloat16)
        target = out_ref.at[:, pl.ds(part * depth, depth)]
        copies.append(pltpu.make_async_copy(held.at[part], target, sems.at[part]))
        copies[-1].start()
    for copy in copies:
        copy.wait()


def store_kernel(new1_ref, new2_ref, new_ref, out1_ref, out2_ref, out_ref, sems):
    pairs = ((new1_ref, out1_ref), (new2_ref, out2_ref), (new_ref, out_ref))
    copies = [pltpu.make_async_copy(*pair, sems.at[i]) for i, pair in enumerate(pairs)]
    for copy in copies:
        copy.start()
    for copy in copies:
        copy.wait()


def places(rows):
    place = lax.broadcasted_iota(jnp.int32, (rows, LANES), 0) * LANES
    return place + lax.broadcasted_iota(jnp.int32, (rows, LANES), 1)


def total_of(pieces, part):
    total = pieces[0][part, :].astype(jnp.float32)
    for piece in pieces[1:]:
        total = total + piece[part, :].astype(jnp.float32)
    return total


def segment_rows(squares, table, bounds):
    rows = math.gcd(squares.shape[0], TILE)
    size = rows * LANES
    place = places(rows)
    table[...] = jnp.zeros_like(table)
    count = bounds.shape[0] - 3

    def segment(k, carry):
        low, high = bounds[k], bounds[k + 1]

        def step(t, total):
            piece = squares[pl.ds(pl.multiple_of(t * rows, rows), rows), :]
            at = t * size
            inside = (place >= low - at) & (place < high - at)
            return total + jnp.where(inside, piece, 0.0)

        total = lax.fori_loop(
            low // size,
            (high + (size - 1)) // size,
            step,
            jnp.zeros((rows, LANES), jnp.float32),
        )
        table[pl.ds(k, 1), :] = jnp.sum(total, axis=0, keepdims=True)
        return carry

    lax.fori_loop(bounds[count + 1], bounds[count + 2], segment, 0)


def early_kernel(n, lengths_ref, weights_hbm, moment1_hbm, moment2_hbm, *rest):
    pieces = rest[:n]
    weights_ref, moment1_ref, moment2_ref, partial_ref, sums_ref, bounds_ref = rest[n : n + 6]
    squares, table, sems = rest[n + 6 :]
    chunks = weights_ref.shape[0]
    pairs = ((weights_hbm, weights_ref), (moment1_hbm, moment1_ref), (moment2_hbm, moment2_ref))
    copies = [pltpu.make_async_copy(*pair, sems.at[i]) for i, pair in enumerate(pairs)]
    for copy in copies:
        copy.start()
    width = chunks * LANES
    count = lengths_ref.shape[0]
    index = lax.axis_index("shard") * lax.axis_size("tensor") + lax.axis_index("tensor")
    base = index * width

    def walk(k, carry):
        at, first, last = carry
        bounds_ref[k] = jnp.clip(at, 0, width)
        then = at + lengths_ref[k]
        first = jnp.where(then <= 0, k + 1, first)
        last = jnp.where(at < width, k + 1, last)
        return (then, first, last)

    at, first, last = lax.fori_loop(
        0, count, walk, (-base, jnp.int32(0), jnp.int32(0))
    )
    bounds_ref[count] = jnp.clip(at, 0, width)
    bounds_ref[count + 1] = first
    bounds_ref[count + 2] = last
    rows = math.gcd(chunks, TILE)

    def add(t, carry):
        part = pl.ds(pl.multiple_of(t * rows, rows), rows)
        partial_ref[part, :] = total_of(pieces, part)
        return carry

    lax.fori_loop(0, chunks // rows, add, 0)
    for copy in copies:
        copy.wait()
    squares[...] = weights_ref[...] * weights_ref[...]
    segment_rows(squares, table, bounds_ref)
    sums_ref[...] = jnp.sum(table[...].T, axis=0, keepdims=True)


def update_kernel(n, step_ref, bounds_ref, sums_ref, weights_ref, moment1_ref, moment2_ref, *rest):
    partial_ref, pieces = rest[0], rest[1 : n + 1]
    rest = rest[1:]
    new1_ref, new2_ref, update_ref, send_ref = rest[n : n + 4]
    squares, table = rest[n + 4 :]

    def power(base):
        return lax.fori_loop(
            0, step_ref[0], lambda i, p: p * base, jnp.full((8, LANES), 1.0, jnp.float32)
        )

    scale1 = (1.0 / (1.0 - power(jnp.float32(0.9))))[0:1, :]
    scale2 = (1.0 / (1.0 - power(jnp.float32(0.999))))[0:1, :]
    chunks = weights_ref.shape[0]
    rows = math.gcd(chunks, TILE)

    def block(t, carry):
        part = pl.ds(pl.multiple_of(t * rows, rows), rows)
        grad = partial_ref[part, :] + total_of(pieces, part)
        new1 = 0.9 * moment1_ref[part, :] + 0.1 * grad
        new2 = 0.999 * moment2_ref[part, :] + 0.001 * grad * grad
        new1_ref[part, :] = new1
        new2_ref[part, :] = new2
        update = (new1 * scale1) / (jnp.sqrt(new2 * scale2) + 1e-06)
        update = update + 0.1 * weights_ref[part, :]
        update_ref[part, :] = update
        squares[part, :] = update * update
        return carry

    lax.fori_loop(0, chunks // rows, block, 0, unroll=2)
    segment_rows(squares, table, bounds_ref)
    mine = jnp.sum(table[...].T, axis=0, keepdims=True)
    which = lax.broadcasted_iota(jnp.int32, (2, LANES), 0)
    both = jnp.where(which == 0, sums_ref[...], mine)
    send_ref[...] = jnp.broadcast_to(both[None], send_ref.shape)


def weights_out_kernel(
    bounds_ref, sums_ref, weights_ref, update_ref, new_ref, narrow_ref, table
):
    chunks = weights_ref.shape[0]
    rows = math.gcd(chunks, TILE)
    size = rows * LANES
    place = places(rows)
    count = bounds_ref.shape[0] - 3
    both = jnp.sum(sums_ref[...], axis=0)
    ratio = 0.25 * (jnp.sqrt(both[0:1, :]) / jnp.maximum(jnp.sqrt(both[1:2, :]), 1.0))
    table[...] = jnp.broadcast_to(ratio, (LANES, LANES)).T

    def segment(k, carry):
        low, high = bounds_ref[k], bounds_ref[k + 1]
        scale = table[pl.ds(k, 1), :]

        def step(t, carry):
            part = pl.ds(pl.multiple_of(t * rows, rows), rows)
            new = weights_ref[part, :] - scale * update_ref[part, :]
            new = jnp.where(place >= low - t * size, new, new_ref[part, :])
            new_ref[part, :] = new
            narrow_ref[part, :] = new.astype(jnp.bfloat16)
            return carry

        return lax.fori_loop(low // size, (high + (size - 1)) // size, step, carry)

    lax.fori_loop(bounds_ref[count + 1], bounds_ref[count + 2], segment, 0)


def exchange_order(n):
    first = [k for k in ORDER if k < n]
    return first + [k for k in range(1, n) if k not in first]


def swap(value, axis, size, k):
    return lax.ppermute(value, axis, [(i, i ^ k) for i in range(size)])


def local(step, lengths, grads, weights, moment1, moment2):
    n = lax.axis_size("shard")
    everyone = n * lax.axis_size("tensor")
    width = weights.shape[0]
    chunks = width // LANES
    count = lengths.shape[0]
    flat = lambda dtype: jax.ShapeDtypeStruct((chunks, LANES), dtype)
    rows = grads.reshape(n // 8, 8, chunks, LANES).transpose(0, 2, 1, 3)
    parts = math.gcd(PARTS, chunks // 16)
    depth = chunks // parts
    staging = [
        pltpu.VMEM((parts, n // 8, depth, 8, LANES), jnp.bfloat16),
        pltpu.VMEM((parts, n * depth, LANES), jnp.float32),
        pltpu.SemaphoreType.DMA((parts,)),
    ]
    pieces = pl.pallas_call(
        functools.partial(split_kernel, n, chunks),
        out_shape=[flat(jnp.bfloat16)] * n,
        in_specs=[HBM],
        out_specs=[VMEM] * n,
        scratch_shapes=staging,
        compiler_params=BIG,
        name="split",
    )(pltpu.with_memory_space_constraint(rows, pltpu.HBM))
    order = exchange_order(n)
    pieces = [pieces[0]] + [swap(pieces[k], "shard", n, k) for k in order]
    early, late = pieces[: EARLY + 1], pieces[EARLY + 1 :]
    square_table = [
        pltpu.VMEM((chunks, LANES), jnp.float32),
        pltpu.VMEM((LANES, LANES), jnp.float32),
    ]
    stored = [
        pltpu.with_memory_space_constraint(value.reshape(chunks, LANES), pltpu.HBM)
        for value in (weights, moment1, moment2)
    ]
    weights, moment1, moment2, partial, sums, bounds = pl.pallas_call(
        functools.partial(early_kernel, len(early)),
        out_shape=[flat(jnp.float32)] * 4
        + [
            jax.ShapeDtypeStruct((1, LANES), jnp.float32),
            jax.ShapeDtypeStruct((count + 3,), jnp.int32),
        ],
        in_specs=[SMEM] + [HBM] * 3 + [VMEM] * len(early),
        out_specs=[VMEM] * 5 + [SMEM],
        scratch_shapes=square_table + [pltpu.SemaphoreType.DMA((3,))],
        compiler_params=BIG,
        cost_estimate=pl.CostEstimate(
            flops=8 * width, bytes_accessed=24 * width, transcendentals=0
        ),
        name="early",
    )(lengths, *stored, *early)
    new1, new2, update, send = pl.pallas_call(
        functools.partial(update_kernel, len(late)),
        out_shape=[flat(jnp.float32)] * 3
        + [jax.ShapeDtypeStruct((everyone, 2, LANES), jnp.float32)],
        in_specs=[SMEM, SMEM] + [VMEM] * (5 + len(late)),
        out_specs=[VMEM] * 4,
        scratch_shapes=square_table,
        compiler_params=BIG,
        name="update",
    )(step, bounds, sums, weights, moment1, moment2, partial, *late)
    sums = lax.all_to_all(send, ("shard", "tensor"), 0, 0, tiled=True)
    new, narrow = pl.pallas_call(
        weights_out_kernel,
        out_shape=[flat(jnp.float32), flat(jnp.bfloat16)],
        in_specs=[SMEM, VMEM, VMEM, VMEM],
        out_specs=[VMEM] * 2,
        scratch_shapes=[pltpu.VMEM((LANES, LANES), jnp.float32)],
        compiler_params=BIG,
        name="new_weights",
    )(bounds, sums, weights, update)
    gathered = {0: narrow}
    for k in range(2, n, 2):
        gathered[k] = swap(narrow, "shard", n, k)
    new1, new2, new = pl.pallas_call(
        store_kernel,
        out_shape=[flat(jnp.float32)] * 3,
        in_specs=[VMEM] * 3,
        out_specs=[HBM] * 3,
        scratch_shapes=[pltpu.SemaphoreType.DMA((3,))],
        compiler_params=BIG,
        cost_estimate=pl.CostEstimate(flops=0, bytes_accessed=12 * width, transcendentals=0),
        name="store",
    )(new1, new2, new)
    new1, new2, new, own = lax.optimization_barrier((new1, new2, new, narrow))
    gathered[1] = swap(own, "shard", n, 1)
    for k in range(2, n, 2):
        gathered[k + 1] = swap(gathered[k], "shard", n, 1)
    soon, last = [0, 1, *range(2, n, 2)], list(range(3, n, 2))
    wide = jax.ShapeDtypeStruct((parts, n * depth, LANES), jnp.float32)
    laid = pl.pallas_call(
        functools.partial(lay_kernel, soon),
        out_shape=wide,
        in_specs=[VMEM] * len(soon),
        out_specs=VMEM,
        compiler_params=BIG,
        cost_estimate=pl.CostEstimate(
            flops=0, bytes_accessed=6 * width * len(soon), transcendentals=0
        ),
        name="lay",
    )(*[gathered[k] for k in soon])
    joined, unused = pl.pallas_call(
        functools.partial(join_kernel, last),
        out_shape=[jax.ShapeDtypeStruct((n // 8, chunks, 8, LANES), jnp.bfloat16), wide],
        in_specs=[VMEM] * (1 + len(last)),
        out_specs=[HBM, VMEM],
        input_output_aliases={0: 1},
        scratch_shapes=[staging[0], staging[2]],
        compiler_params=BIG,
        name="join",
    )(laid, *[gathered[k] for k in last])
    train = joined.transpose(0, 2, 1, 3).reshape(n, 1, width)
    return (new.reshape(width), new1.reshape(width), new2.reshape(width), train)


def solution(mesh):
    whole = P(("shard", "tensor"))
    return jax.shard_map(
        local,
        mesh=mesh,
        in_specs=(P(), P(), P("shard", None, "tensor", None), whole, whole, whole),
        out_specs=(whole, whole, whole, P(None, "tensor", None)),
        check_vma=False,
    )
```

```python
import functools
import math

import jax
import jax.numpy as jnp
from jax import lax
from jax.experimental import pallas as pl
from jax.experimental.pallas import tpu as pltpu
from jax.sharding import PartitionSpec as P

LANES = 128
TILE = 64
PARTS = 4
ORDER = (2, 4, 3, 5, 6, 7, 1)
EARLY = 3
VMEM = pl.BlockSpec(memory_space=pltpu.VMEM)
SMEM = pl.BlockSpec(memory_space=pltpu.SMEM)
HBM = pl.BlockSpec(memory_space=pltpu.HBM)
BIG = pltpu.CompilerParams(vmem_limit_bytes=48 << 20)


def split_kernel(n, chunks, grads_ref, *rest):
    outs, (held, wide, sems) = rest[:n], rest[n:]
    me = lax.axis_index("shard")
    parts, depth = held.shape[0], held.shape[2]
    copies = []
    for part in range(parts):
        source = grads_ref.at[:, pl.ds(part * depth, depth)]
        copies.append(pltpu.make_async_copy(source, held.at[part], sems.at[part]))
        copies[-1].start()
    for part in range(parts):
        copies[part].wait()
        wide[part] = held[part].astype(jnp.float32).reshape(wide.shape[1:])
        for k in range(n):
            row = me ^ k
            first = (row // 8) * (depth * 8) + row % 8
            taken = wide[part, pl.ds(first, depth, stride=8), :]
            outs[k][part * depth : (part + 1) * depth, :] = taken.astype(jnp.bfloat16)


def lay(rows, wide, part, depth, ins):
    me = lax.axis_index("shard")
    for k, value in zip(rows, ins):
        row = me ^ k
        first = (row // 8) * (depth * 8) + row % 8
        taken = value[part * depth : (part + 1) * depth, :]
        wide[part, pl.ds(first, depth, stride=8), :] = taken.astype(jnp.float32)


def lay_kernel(rows, *rest):
    ins, wide = rest[:-1], rest[-1]
    parts = wide.shape[0]
    for part in range(parts):
        lay(rows, wide, part, ins[0].shape[0] // parts, ins)


def join_kernel(rows, *rest):
    ins, (out_ref, wide, held, sems) = rest[1:-4], rest[-4:]
    parts, depth = held.shape[0], held.shape[2]
    copies = []
    for part in range(parts):
        lay(rows, wide, part, depth, ins)
        held[part] = wide[part].reshape(held.shape[1:]).astype(jnp.bfloat16)
        target = out_ref.at[:, pl.ds(part * depth, depth)]
        copies.append(pltpu.make_async_copy(held.at[part], target, sems.at[part]))
        copies[-1].start()
    for copy in copies:
        copy.wait()


def store_kernel(new1_ref, new2_ref, new_ref, out1_ref, out2_ref, out_ref, sems):
    pairs = ((new1_ref, out1_ref), (new2_ref, out2_ref), (new_ref, out_ref))
    copies = [pltpu.make_async_copy(*pair, sems.at[i]) for i, pair in enumerate(pairs)]
    for copy in copies:
        copy.start()
    for copy in copies:
        copy.wait()


def places(rows):
    place = lax.broadcasted_iota(jnp.int32, (rows, LANES), 0) * LANES
    return place + lax.broadcasted_iota(jnp.int32, (rows, LANES), 1)


def total_of(pieces, part):
    total = pieces[0][part, :].astype(jnp.float32)
    for piece in pieces[1:]:
        total = total + piece[part, :].astype(jnp.float32)
    return total


def segment_rows(squares, table, bounds):
    rows = math.gcd(squares.shape[0], TILE)
    size = rows * LANES
    place = places(rows)
    table[...] = jnp.zeros_like(table)
    count = bounds.shape[0] - 3

    def segment(k, carry):
        low, high = bounds[k], bounds[k + 1]

        def step(t, total):
            piece = squares[pl.ds(pl.multiple_of(t * rows, rows), rows), :]
            at = t * size
            inside = (place >= low - at) & (place < high - at)
            return total + jnp.where(inside, piece, 0.0)

        total = lax.fori_loop(
            low // size,
            (high + (size - 1)) // size,
            step,
            jnp.zeros((rows, LANES), jnp.float32),
        )
        table[pl.ds(k, 1), :] = jnp.sum(total, axis=0, keepdims=True)
        return carry

    lax.fori_loop(bounds[count + 1], bounds[count + 2], segment, 0)


def early_kernel(n, step_ref, lengths_ref, weights_hbm, moment1_hbm, moment2_hbm, *rest):
    pieces = rest[:n]
    weights_ref, moment1_ref, moment2_ref, partial_ref, sums_ref, scales_ref = rest[n : n + 6]
    bounds_ref, squares, table, sems = rest[n + 6 :]
    chunks = weights_ref.shape[0]
    pairs = ((weights_hbm, weights_ref), (moment1_hbm, moment1_ref), (moment2_hbm, moment2_ref))
    copies = [pltpu.make_async_copy(*pair, sems.at[i]) for i, pair in enumerate(pairs)]
    for copy in copies:
        copy.start()
    width = chunks * LANES
    count = lengths_ref.shape[0]
    index = lax.axis_index("shard") * lax.axis_size("tensor") + lax.axis_index("tensor")
    base = index * width

    def walk(k, carry):
        at, first, last = carry
        bounds_ref[k] = jnp.clip(at, 0, width)
        then = at + lengths_ref[k]
        first = jnp.where(then <= 0, k + 1, first)
        last = jnp.where(at < width, k + 1, last)
        return (then, first, last)

    at, first, last = lax.fori_loop(
        0, count, walk, (-base, jnp.int32(0), jnp.int32(0))
    )
    bounds_ref[count] = jnp.clip(at, 0, width)
    bounds_ref[count + 1] = first
    bounds_ref[count + 2] = last
    rows = math.gcd(chunks, TILE)

    def add(t, carry):
        part = pl.ds(pl.multiple_of(t * rows, rows), rows)
        partial_ref[part, :] = total_of(pieces, part)
        return carry

    lax.fori_loop(0, chunks // rows, add, 0)

    def power(base):
        return lax.fori_loop(
            0, step_ref[0], lambda i, p: p * base, jnp.full((1, LANES), 1.0, jnp.float32)
        )

    scales_ref[0:1, :] = 1.0 / (1.0 - power(jnp.float32(0.9)))
    scales_ref[1:2, :] = 1.0 / (1.0 - power(jnp.float32(0.999)))
    for copy in copies:
        copy.wait()
    squares[...] = weights_ref[...] * weights_ref[...]
    segment_rows(squares, table, bounds_ref)
    sums_ref[...] = jnp.sum(table[...].T, axis=0, keepdims=True)


def update_kernel(n, bounds_ref, scales_ref, sums_ref, weights_ref, moment1_ref, moment2_ref, *rest):
    partial_ref, pieces = rest[0], rest[1 : n + 1]
    rest = rest[1:]
    new1_ref, new2_ref, update_ref, send_ref = rest[n : n + 4]
    squares, table = rest[n + 4 :]

    scale1, scale2 = scales_ref[0:1, :], scales_ref[1:2, :]
    chunks = weights_ref.shape[0]
    rows = math.gcd(chunks, TILE)

    def block(t, carry):
        part = pl.ds(pl.multiple_of(t * rows, rows), rows)
        grad = partial_ref[part, :] + total_of(pieces, part)
        new1 = 0.9 * moment1_ref[part, :] + 0.1 * grad
        new2 = 0.999 * moment2_ref[part, :] + 0.001 * grad * grad
        new1_ref[part, :] = new1
        new2_ref[part, :] = new2
        update = (new1 * scale1) / (jnp.sqrt(new2 * scale2) + 1e-06)
        update = update + 0.1 * weights_ref[part, :]
        update_ref[part, :] = update
        squares[part, :] = update * update
        return carry

    lax.fori_loop(0, chunks // rows, block, 0, unroll=2)
    segment_rows(squares, table, bounds_ref)
    mine = jnp.sum(table[...].T, axis=0, keepdims=True)
    half = (send_ref.shape[0], LANES)
    send_ref[:, :LANES] = jnp.broadcast_to(sums_ref[...], half)
    send_ref[:, LANES:] = jnp.broadcast_to(mine, half)


def weights_out_kernel(
    bounds_ref, sums_ref, weights_ref, update_ref, new_ref, narrow_ref, table
):
    chunks = weights_ref.shape[0]
    rows = math.gcd(chunks, TILE)
    size = rows * LANES
    place = places(rows)
    count = bounds_ref.shape[0] - 3
    both = jnp.sum(sums_ref[...], axis=0, keepdims=True)
    ratio = jnp.sqrt(both[:, :LANES]) / jnp.maximum(jnp.sqrt(both[:, LANES:]), 1.0)
    ratio = 0.25 * ratio
    table[...] = jnp.broadcast_to(ratio, (LANES, LANES)).T

    def segment(k, carry):
        low, high = bounds_ref[k], bounds_ref[k + 1]
        scale = table[pl.ds(k, 1), :]

        def step(t, carry):
            part = pl.ds(pl.multiple_of(t * rows, rows), rows)
            new = weights_ref[part, :] - scale * update_ref[part, :]
            new = jnp.where(place >= low - t * size, new, new_ref[part, :])
            new_ref[part, :] = new
            narrow_ref[part, :] = new.astype(jnp.bfloat16)
            return carry

        return lax.fori_loop(low // size, (high + (size - 1)) // size, step, carry)

    lax.fori_loop(bounds_ref[count + 1], bounds_ref[count + 2], segment, 0)


def exchange_order(n):
    first = [k for k in ORDER if k < n]
    return first + [k for k in range(1, n) if k not in first]


def swap(value, axis, size, k):
    return lax.ppermute(value, axis, [(i, i ^ k) for i in range(size)])


def local(step, lengths, grads, weights, moment1, moment2):
    n = lax.axis_size("shard")
    everyone = n * lax.axis_size("tensor")
    width = weights.shape[0]
    chunks = width // LANES
    count = lengths.shape[0]
    flat = lambda dtype: jax.ShapeDtypeStruct((chunks, LANES), dtype)
    rows = grads.reshape(n // 8, 8, chunks, LANES).transpose(0, 2, 1, 3)
    parts = math.gcd(PARTS, chunks // 16)
    depth = chunks // parts
    staging = [
        pltpu.VMEM((parts, n // 8, depth, 8, LANES), jnp.bfloat16),
        pltpu.VMEM((parts, n * depth, LANES), jnp.float32),
        pltpu.SemaphoreType.DMA((parts,)),
    ]
    pieces = pl.pallas_call(
        functools.partial(split_kernel, n, chunks),
        out_shape=[flat(jnp.bfloat16)] * n,
        in_specs=[HBM],
        out_specs=[VMEM] * n,
        scratch_shapes=staging,
        compiler_params=BIG,
        name="split",
    )(pltpu.with_memory_space_constraint(rows, pltpu.HBM))
    order = exchange_order(n)
    pieces = [pieces[0]] + [swap(pieces[k], "shard", n, k) for k in order]
    early, late = pieces[: EARLY + 1], pieces[EARLY + 1 :]
    square_table = [
        pltpu.VMEM((chunks, LANES), jnp.float32),
        pltpu.VMEM((LANES, LANES), jnp.float32),
    ]
    stored = [
        pltpu.with_memory_space_constraint(value.reshape(chunks, LANES), pltpu.HBM)
        for value in (weights, moment1, moment2)
    ]
    weights, moment1, moment2, partial, sums, scales, bounds = pl.pallas_call(
        functools.partial(early_kernel, len(early)),
        out_shape=[flat(jnp.float32)] * 4
        + [
            jax.ShapeDtypeStruct((1, LANES), jnp.float32),
            jax.ShapeDtypeStruct((2, LANES), jnp.float32),
            jax.ShapeDtypeStruct((count + 3,), jnp.int32),
        ],
        in_specs=[SMEM] * 2 + [HBM] * 3 + [VMEM] * len(early),
        out_specs=[VMEM] * 6 + [SMEM],
        scratch_shapes=square_table + [pltpu.SemaphoreType.DMA((3,))],
        compiler_params=BIG,
        cost_estimate=pl.CostEstimate(
            flops=8 * width, bytes_accessed=24 * width, transcendentals=0
        ),
        name="early",
    )(step, lengths, *stored, *early)
    new1, new2, update, send = pl.pallas_call(
        functools.partial(update_kernel, len(late)),
        out_shape=[flat(jnp.float32)] * 3
        + [jax.ShapeDtypeStruct((everyone, 2 * LANES), jnp.float32)],
        in_specs=[SMEM] + [VMEM] * (6 + len(late)),
        out_specs=[VMEM] * 4,
        scratch_shapes=square_table,
        compiler_params=BIG,
        name="update",
    )(bounds, scales, sums, weights, moment1, moment2, partial, *late)
    sums = lax.all_to_all(send, ("shard", "tensor"), 0, 0, tiled=True)
    new, narrow = pl.pallas_call(
        weights_out_kernel,
        out_shape=[flat(jnp.float32), flat(jnp.bfloat16)],
        in_specs=[SMEM, VMEM, VMEM, VMEM],
        out_specs=[VMEM] * 2,
        scratch_shapes=[pltpu.VMEM((LANES, LANES), jnp.float32)],
        compiler_params=BIG,
        name="new_weights",
    )(bounds, sums, weights, update)
    gathered = {0: narrow}
    for k in range(2, n, 2):
        gathered[k] = swap(narrow, "shard", n, k)
    new1, new2, new = pl.pallas_call(
        store_kernel,
        out_shape=[flat(jnp.float32)] * 3,
        in_specs=[VMEM] * 3,
        out_specs=[HBM] * 3,
        scratch_shapes=[pltpu.SemaphoreType.DMA((3,))],
        compiler_params=BIG,
        cost_estimate=pl.CostEstimate(flops=0, bytes_accessed=12 * width, transcendentals=0),
        name="store",
    )(new1, new2, new)
    new1, new2, new, own = lax.optimization_barrier((new1, new2, new, narrow))
    gathered[1] = swap(own, "shard", n, 1)
    for k in range(2, n, 2):
        gathered[k + 1] = swap(gathered[k], "shard", n, 1)
    soon, last = [0, 1, *range(2, n, 2)], list(range(3, n, 2))
    wide = jax.ShapeDtypeStruct((parts, n * depth, LANES), jnp.float32)
    laid = pl.pallas_call(
        functools.partial(lay_kernel, soon),
        out_shape=wide,
        in_specs=[VMEM] * len(soon),
        out_specs=VMEM,
        compiler_params=BIG,
        cost_estimate=pl.CostEstimate(
            flops=0, bytes_accessed=6 * width * len(soon), transcendentals=0
        ),
        name="lay",
    )(*[gathered[k] for k in soon])
    joined, unused = pl.pallas_call(
        functools.partial(join_kernel, last),
        out_shape=[jax.ShapeDtypeStruct((n // 8, chunks, 8, LANES), jnp.bfloat16), wide],
        in_specs=[VMEM] * (1 + len(last)),
        out_specs=[HBM, VMEM],
        input_output_aliases={0: 1},
        scratch_shapes=[staging[0], staging[2]],
        compiler_params=BIG,
        name="join",
    )(laid, *[gathered[k] for k in last])
    train = joined.transpose(0, 2, 1, 3).reshape(n, 1, width)
    return (new.reshape(width), new1.reshape(width), new2.reshape(width), train)


def solution(mesh):
    whole = P(("shard", "tensor"))
    return jax.shard_map(
        local,
        mesh=mesh,
        in_specs=(P(), P(), P("shard", None, "tensor", None), whole, whole, whole),
        out_specs=(whole, whole, whole, P(None, "tensor", None)),
        check_vma=False,
    )
```

```python
import functools
import math

import jax
import jax.numpy as jnp
from jax import lax
from jax.experimental import pallas as pl
from jax.experimental.pallas import tpu as pltpu
from jax.sharding import PartitionSpec as P

LANES = 128
TILE = 64
PARTS = 8
ORDER = (2, 4, 3, 5, 6, 7, 1)
EARLY = 3
VMEM = pl.BlockSpec(memory_space=pltpu.VMEM)
SMEM = pl.BlockSpec(memory_space=pltpu.SMEM)
HBM = pl.BlockSpec(memory_space=pltpu.HBM)
BIG = pltpu.CompilerParams(vmem_limit_bytes=48 << 20)


def split_kernel(n, chunks, grads_ref, *rest):
    outs, (held, wide, sems) = rest[:n], rest[n:]
    me = lax.axis_index("shard")
    parts, depth = held.shape[0], held.shape[2]
    copies = []
    for part in range(parts):
        source = grads_ref.at[:, pl.ds(part * depth, depth)]
        copies.append(pltpu.make_async_copy(source, held.at[part], sems.at[part]))
        copies[-1].start()
    for part in range(parts):
        copies[part].wait()
        wide[part] = held[part].astype(jnp.float32).reshape(wide.shape[1:])
        for k in range(n):
            row = me ^ k
            first = (row // 8) * (depth * 8) + row % 8
            taken = wide[part, pl.ds(first, depth, stride=8), :]
            outs[k][part * depth : (part + 1) * depth, :] = taken.astype(jnp.bfloat16)


def lay(rows, wide, part, depth, ins):
    me = lax.axis_index("shard")
    for k, value in zip(rows, ins):
        row = me ^ k
        first = (row // 8) * (depth * 8) + row % 8
        taken = value[part * depth : (part + 1) * depth, :]
        wide[part, pl.ds(first, depth, stride=8), :] = taken.astype(jnp.float32)


def lay_kernel(rows, *rest):
    ins, wide = rest[:-1], rest[-1]
    parts = wide.shape[0]
    for part in range(parts):
        lay(rows, wide, part, ins[0].shape[0] // parts, ins)


def join_kernel(rows, *rest):
    ins, (out_ref, wide, held, sems) = rest[1:-4], rest[-4:]
    parts, depth = held.shape[0], held.shape[2]
    copies = []
    for part in range(parts):
        lay(rows, wide, part, depth, ins)
        held[part] = wide[part].reshape(held.shape[1:]).astype(jnp.bfloat16)
        target = out_ref.at[:, pl.ds(part * depth, depth)]
        copies.append(pltpu.make_async_copy(held.at[part], target, sems.at[part]))
        copies[-1].start()
    for copy in copies:
        copy.wait()


def places(rows):
    place = lax.broadcasted_iota(jnp.int32, (rows, LANES), 0) * LANES
    return place + lax.broadcasted_iota(jnp.int32, (rows, LANES), 1)


def total_of(pieces, part):
    total = pieces[0][part, :].astype(jnp.float32)
    for piece in pieces[1:]:
        total = total + piece[part, :].astype(jnp.float32)
    return total


def segment_rows(squares, table, bounds):
    rows = math.gcd(squares.shape[0], TILE)
    size = rows * LANES
    place = places(rows)
    table[...] = jnp.zeros_like(table)
    count = bounds.shape[0] - 3

    def segment(k, carry):
        low, high = bounds[k], bounds[k + 1]

        def step(t, total):
            piece = squares[pl.ds(pl.multiple_of(t * rows, rows), rows), :]
            at = t * size
            inside = (place >= low - at) & (place < high - at)
            return total + jnp.where(inside, piece, 0.0)

        total = lax.fori_loop(
            low // size,
            (high + (size - 1)) // size,
            step,
            jnp.zeros((rows, LANES), jnp.float32),
        )
        table[pl.ds(k, 1), :] = jnp.sum(total, axis=0, keepdims=True)
        return carry

    lax.fori_loop(bounds[count + 1], bounds[count + 2], segment, 0)


def early_kernel(n, step_ref, lengths_ref, weights_hbm, moment1_hbm, moment2_hbm, *rest):
    pieces = rest[:n]
    weights_ref, moment1_ref, moment2_ref, partial_ref, sums_ref, scales_ref = rest[n : n + 6]
    bounds_ref, squares, table, sems = rest[n + 6 :]
    chunks = weights_ref.shape[0]
    pairs = ((weights_hbm, weights_ref), (moment1_hbm, moment1_ref), (moment2_hbm, moment2_ref))
    copies = [pltpu.make_async_copy(*pair, sems.at[i]) for i, pair in enumerate(pairs)]
    for copy in copies:
        copy.start()
    width = chunks * LANES
    count = lengths_ref.shape[0]
    index = lax.axis_index("shard") * lax.axis_size("tensor") + lax.axis_index("tensor")
    base = index * width

    def walk(k, carry):
        at, first, last = carry
        bounds_ref[k] = jnp.clip(at, 0, width)
        then = at + lengths_ref[k]
        first = jnp.where(then <= 0, k + 1, first)
        last = jnp.where(at < width, k + 1, last)
        return (then, first, last)

    at, first, last = lax.fori_loop(
        0, count, walk, (-base, jnp.int32(0), jnp.int32(0))
    )
    bounds_ref[count] = jnp.clip(at, 0, width)
    bounds_ref[count + 1] = first
    bounds_ref[count + 2] = last
    rows = math.gcd(chunks, TILE)

    def add(t, carry):
        part = pl.ds(pl.multiple_of(t * rows, rows), rows)
        partial_ref[part, :] = total_of(pieces, part)
        return carry

    lax.fori_loop(0, chunks // rows, add, 0)

    def power(base):
        return lax.fori_loop(
            0, step_ref[0], lambda i, p: p * base, jnp.full((1, LANES), 1.0, jnp.float32)
        )

    scales_ref[0:1, :] = 1.0 / (1.0 - power(jnp.float32(0.9)))
    scales_ref[1:2, :] = 1.0 / (1.0 - power(jnp.float32(0.999)))
    for copy in copies:
        copy.wait()
    squares[...] = weights_ref[...] * weights_ref[...]
    segment_rows(squares, table, bounds_ref)
    sums_ref[...] = jnp.sum(table[...].T, axis=0, keepdims=True)


def update_kernel(n, bounds_ref, scales_ref, sums_ref, weights_ref, moment1_ref, moment2_ref, *rest):
    partial_ref, pieces = rest[0], rest[1 : n + 1]
    rest = rest[1:]
    new1_ref, new2_ref, update_ref, send_ref = rest[n : n + 4]
    squares, table = rest[n + 4 :]

    scale1, scale2 = scales_ref[0:1, :], scales_ref[1:2, :]
    chunks = weights_ref.shape[0]
    rows = math.gcd(chunks, TILE)

    def block(t, carry):
        part = pl.ds(pl.multiple_of(t * rows, rows), rows)
        grad = partial_ref[part, :] + total_of(pieces, part)
        new1 = 0.9 * moment1_ref[part, :] + 0.1 * grad
        new2 = 0.999 * moment2_ref[part, :] + 0.001 * grad * grad
        new1_ref[part, :] = new1
        new2_ref[part, :] = new2
        update = (new1 * scale1) / (jnp.sqrt(new2 * scale2) + 1e-06)
        update = update + 0.1 * weights_ref[part, :]
        update_ref[part, :] = update
        squares[part, :] = update * update
        return carry

    lax.fori_loop(0, chunks // rows, block, 0, unroll=2)
    segment_rows(squares, table, bounds_ref)
    mine = jnp.sum(table[...].T, axis=0, keepdims=True)
    half = (send_ref.shape[0], LANES)
    send_ref[:, :LANES] = jnp.broadcast_to(sums_ref[...], half)
    send_ref[:, LANES:] = jnp.broadcast_to(mine, half)


def scaled(bounds, table, weights, update, write):
    chunks = weights.shape[0]
    rows = math.gcd(chunks, TILE)
    size = rows * LANES
    place = places(rows)
    count = bounds.shape[0] - 3

    def segment(k, carry):
        low, high = bounds[k], bounds[k + 1]
        scale = table[pl.ds(k, 1), :]

        def step(t, carry):
            part = pl.ds(pl.multiple_of(t * rows, rows), rows)
            new = weights[part, :] - scale * update[part, :]
            write(part, place >= low - t * size, new)
            return carry

        return lax.fori_loop(low // size, (high + (size - 1)) // size, step, carry)

    lax.fori_loop(bounds[count + 1], bounds[count + 2], segment, 0)


def narrow_kernel(bounds_ref, sums_ref, weights_ref, update_ref, narrow_ref, table):
    both = jnp.sum(sums_ref[...], axis=0, keepdims=True)
    ratio = jnp.sqrt(both[:, :LANES]) / jnp.maximum(jnp.sqrt(both[:, LANES:]), 1.0)
    ratio = 0.25 * ratio
    table[...] = jnp.broadcast_to(ratio, (LANES, LANES)).T

    def write(part, mine, new):
        new = jnp.where(mine, new, narrow_ref[part, :].astype(jnp.float32))
        narrow_ref[part, :] = new.astype(jnp.bfloat16)

    scaled(bounds_ref, table, weights_ref, update_ref, write)


def store_kernel(bounds_ref, table, weights_ref, update_ref, new1_ref, new2_ref, *rest):
    out1_ref, out2_ref, out_ref, new_ref, sems = rest
    pairs = ((new1_ref, out1_ref), (new2_ref, out2_ref), (new_ref, out_ref))
    copies = [pltpu.make_async_copy(*pair, sems.at[i]) for i, pair in enumerate(pairs)]
    copies[0].start()
    copies[1].start()

    def write(part, mine, new):
        new_ref[part, :] = jnp.where(mine, new, new_ref[part, :])

    scaled(bounds_ref, table, weights_ref, update_ref, write)
    copies[2].start()
    for copy in copies:
        copy.wait()


def exchange_order(n):
    first = [k for k in ORDER if k < n]
    return first + [k for k in range(1, n) if k not in first]


def swap(value, axis, size, k):
    return lax.ppermute(value, axis, [(i, i ^ k) for i in range(size)])


def local(step, lengths, grads, weights, moment1, moment2):
    n = lax.axis_size("shard")
    everyone = n * lax.axis_size("tensor")
    width = weights.shape[0]
    chunks = width // LANES
    count = lengths.shape[0]
    flat = lambda dtype: jax.ShapeDtypeStruct((chunks, LANES), dtype)
    rows = grads.reshape(n // 8, 8, chunks, LANES).transpose(0, 2, 1, 3)
    parts = math.gcd(PARTS, chunks // 16)
    depth = chunks // parts
    staging = [
        pltpu.VMEM((parts, n // 8, depth, 8, LANES), jnp.bfloat16),
        pltpu.VMEM((parts, n * depth, LANES), jnp.float32),
        pltpu.SemaphoreType.DMA((parts,)),
    ]
    pieces = pl.pallas_call(
        functools.partial(split_kernel, n, chunks),
        out_shape=[flat(jnp.bfloat16)] * n,
        in_specs=[HBM],
        out_specs=[VMEM] * n,
        scratch_shapes=staging,
        compiler_params=BIG,
        name="split",
    )(pltpu.with_memory_space_constraint(rows, pltpu.HBM))
    order = exchange_order(n)
    pieces = [pieces[0]] + [swap(pieces[k], "shard", n, k) for k in order]
    early, late = pieces[: EARLY + 1], pieces[EARLY + 1 :]
    square_table = [
        pltpu.VMEM((chunks, LANES), jnp.float32),
        pltpu.VMEM((LANES, LANES), jnp.float32),
    ]
    stored = [
        pltpu.with_memory_space_constraint(value.reshape(chunks, LANES), pltpu.HBM)
        for value in (weights, moment1, moment2)
    ]
    weights, moment1, moment2, partial, sums, scales, bounds = pl.pallas_call(
        functools.partial(early_kernel, len(early)),
        out_shape=[flat(jnp.float32)] * 4
        + [
            jax.ShapeDtypeStruct((1, LANES), jnp.float32),
            jax.ShapeDtypeStruct((2, LANES), jnp.float32),
            jax.ShapeDtypeStruct((count + 3,), jnp.int32),
        ],
        in_specs=[SMEM] * 2 + [HBM] * 3 + [VMEM] * len(early),
        out_specs=[VMEM] * 6 + [SMEM],
        scratch_shapes=square_table + [pltpu.SemaphoreType.DMA((3,))],
        compiler_params=BIG,
        cost_estimate=pl.CostEstimate(
            flops=8 * width, bytes_accessed=24 * width, transcendentals=0
        ),
        name="early",
    )(step, lengths, *stored, *early)
    new1, new2, update, send = pl.pallas_call(
        functools.partial(update_kernel, len(late)),
        out_shape=[flat(jnp.float32)] * 3
        + [jax.ShapeDtypeStruct((everyone, 2 * LANES), jnp.float32)],
        in_specs=[SMEM] + [VMEM] * (6 + len(late)),
        out_specs=[VMEM] * 4,
        scratch_shapes=square_table,
        compiler_params=BIG,
        name="update",
    )(bounds, scales, sums, weights, moment1, moment2, partial, *late)
    sums = lax.all_to_all(send, ("shard", "tensor"), 0, 0, tiled=True)
    narrow, table = pl.pallas_call(
        narrow_kernel,
        out_shape=[flat(jnp.bfloat16), jax.ShapeDtypeStruct((LANES, LANES), jnp.float32)],
        in_specs=[SMEM, VMEM, VMEM, VMEM],
        out_specs=[VMEM] * 2,
        compiler_params=BIG,
        name="narrow_weights",
    )(bounds, sums, weights, update)
    gathered = {0: narrow}
    for k in range(2, n, 2):
        gathered[k] = swap(narrow, "shard", n, k)
    new1, new2, new = pl.pallas_call(
        store_kernel,
        out_shape=[flat(jnp.float32)] * 3,
        in_specs=[SMEM] + [VMEM] * 5,
        out_specs=[HBM] * 3,
        scratch_shapes=[
            pltpu.VMEM((chunks, LANES), jnp.float32),
            pltpu.SemaphoreType.DMA((3,)),
        ],
        compiler_params=BIG,
        cost_estimate=pl.CostEstimate(
            flops=4 * width, bytes_accessed=20 * width, transcendentals=0
        ),
        name="store",
    )(bounds, table, weights, update, new1, new2)
    new1, new2, new, own = lax.optimization_barrier((new1, new2, new, narrow))
    gathered[1] = swap(own, "shard", n, 1)
    for k in range(2, n, 2):
        gathered[k + 1] = swap(gathered[k], "shard", n, 1)
    soon, last = [0, 1, *range(2, n, 2)], list(range(3, n, 2))
    wide = jax.ShapeDtypeStruct((parts, n * depth, LANES), jnp.float32)
    laid = pl.pallas_call(
        functools.partial(lay_kernel, soon),
        out_shape=wide,
        in_specs=[VMEM] * len(soon),
        out_specs=VMEM,
        compiler_params=BIG,
        cost_estimate=pl.CostEstimate(
            flops=0, bytes_accessed=6 * width * len(soon), transcendentals=0
        ),
        name="lay",
    )(*[gathered[k] for k in soon])
    joined, unused = pl.pallas_call(
        functools.partial(join_kernel, last),
        out_shape=[jax.ShapeDtypeStruct((n // 8, chunks, 8, LANES), jnp.bfloat16), wide],
        in_specs=[VMEM] * (1 + len(last)),
        out_specs=[HBM, VMEM],
        input_output_aliases={0: 1},
        scratch_shapes=[staging[0], staging[2]],
        compiler_params=BIG,
        name="join",
    )(laid, *[gathered[k] for k in last])
    train = joined.transpose(0, 2, 1, 3).reshape(n, 1, width)
    return (new.reshape(width), new1.reshape(width), new2.reshape(width), train)


def solution(mesh):
    whole = P(("shard", "tensor"))
    return jax.shard_map(
        local,
        mesh=mesh,
        in_specs=(P(), P(), P("shard", None, "tensor", None), whole, whole, whole),
        out_specs=(whole, whole, whole, P(None, "tensor", None)),
        check_vma=False,
    )
```

```python
import functools
import math

import jax
import jax.numpy as jnp
from jax import lax
from jax.experimental import pallas as pl
from jax.experimental.pallas import tpu as pltpu
from jax.sharding import PartitionSpec as P

LANES = 128
TILE = 64
PARTS = 8
ORDER = (2, 4, 3, 5, 6, 7, 1)
EARLY = 3
VMEM = pl.BlockSpec(memory_space=pltpu.VMEM)
SMEM = pl.BlockSpec(memory_space=pltpu.SMEM)
HBM = pl.BlockSpec(memory_space=pltpu.HBM)
BIG = pltpu.CompilerParams(vmem_limit_bytes=48 << 20)


def split_kernel(n, chunks, grads_ref, *rest):
    outs, (held, wide, sems) = rest[:n], rest[n:]
    me = lax.axis_index("shard")
    parts, depth = held.shape[0], held.shape[2]
    copies = []
    for part in range(parts):
        source = grads_ref.at[:, pl.ds(part * depth, depth)]
        copies.append(pltpu.make_async_copy(source, held.at[part], sems.at[part]))
        copies[-1].start()
    for part in range(parts):
        copies[part].wait()
        wide[part] = held[part].astype(jnp.float32).reshape(wide.shape[1:])
        for k in range(n):
            row = me ^ k
            first = (row // 8) * (depth * 8) + row % 8
            taken = wide[part, pl.ds(first, depth, stride=8), :]
            outs[k][part * depth : (part + 1) * depth, :] = taken.astype(jnp.bfloat16)


def lay(rows, wide, part, depth, ins):
    me = lax.axis_index("shard")
    for k, value in zip(rows, ins):
        row = me ^ k
        first = (row // 8) * (depth * 8) + row % 8
        taken = value[part * depth : (part + 1) * depth, :]
        wide[part, pl.ds(first, depth, stride=8), :] = taken.astype(jnp.float32)


def lay_kernel(rows, *rest):
    ins, wide = rest[:-1], rest[-1]
    parts = wide.shape[0]
    for part in range(parts):
        lay(rows, wide, part, ins[0].shape[0] // parts, ins)


def join_kernel(rows, *rest):
    ins, (out_ref, wide, held, sems) = rest[1:-4], rest[-4:]
    parts, depth = held.shape[0], held.shape[2]
    copies = []
    for part in range(parts):
        lay(rows, wide, part, depth, ins)
        held[part] = wide[part].reshape(held.shape[1:]).astype(jnp.bfloat16)
        target = out_ref.at[:, pl.ds(part * depth, depth)]
        copies.append(pltpu.make_async_copy(held.at[part], target, sems.at[part]))
        copies[-1].start()
    for copy in copies:
        copy.wait()


def places(rows):
    place = lax.broadcasted_iota(jnp.int32, (rows, LANES), 0) * LANES
    return place + lax.broadcasted_iota(jnp.int32, (rows, LANES), 1)


def total_of(pieces, part):
    total = pieces[0][part, :].astype(jnp.float32)
    for piece in pieces[1:]:
        total = total + piece[part, :].astype(jnp.float32)
    return total


def segment_rows(squares, table, bounds):
    rows = math.gcd(squares.shape[0], TILE)
    size = rows * LANES
    place = places(rows)
    table[...] = jnp.zeros_like(table)
    count = bounds.shape[0] - 3

    def segment(k, carry):
        low, high = bounds[k], bounds[k + 1]

        def step(t, total):
            piece = squares[pl.ds(pl.multiple_of(t * rows, rows), rows), :]
            at = t * size
            inside = (place >= low - at) & (place < high - at)
            return total + jnp.where(inside, piece, 0.0)

        total = lax.fori_loop(
            low // size,
            (high + (size - 1)) // size,
            step,
            jnp.zeros((rows, LANES), jnp.float32),
        )
        table[pl.ds(k, 1), :] = jnp.sum(total, axis=0, keepdims=True)
        return carry

    lax.fori_loop(bounds[count + 1], bounds[count + 2], segment, 0)


def early_kernel(n, step_ref, lengths_ref, weights_hbm, moment1_hbm, moment2_hbm, *rest):
    pieces = rest[:n]
    weights_ref, moment1_ref, moment2_ref, partial_ref, sums_ref, scales_ref = rest[n : n + 6]
    bounds_ref, squares, table, sems = rest[n + 6 :]
    chunks = weights_ref.shape[0]
    pairs = ((weights_hbm, weights_ref), (moment1_hbm, moment1_ref), (moment2_hbm, moment2_ref))
    copies = [pltpu.make_async_copy(*pair, sems.at[i]) for i, pair in enumerate(pairs)]
    for copy in copies:
        copy.start()
    width = chunks * LANES
    count = lengths_ref.shape[0]
    index = lax.axis_index("shard") * lax.axis_size("tensor") + lax.axis_index("tensor")
    base = index * width

    def walk(k, carry):
        at, first, last = carry
        bounds_ref[k] = jnp.clip(at, 0, width)
        then = at + lengths_ref[k]
        first = jnp.where(then <= 0, k + 1, first)
        last = jnp.where(at < width, k + 1, last)
        return (then, first, last)

    at, first, last = lax.fori_loop(
        0, count, walk, (-base, jnp.int32(0), jnp.int32(0))
    )
    bounds_ref[count] = jnp.clip(at, 0, width)
    bounds_ref[count + 1] = first
    bounds_ref[count + 2] = last
    rows = math.gcd(chunks, TILE)

    def add(t, carry):
        part = pl.ds(pl.multiple_of(t * rows, rows), rows)
        partial_ref[part, :] = total_of(pieces, part)
        return carry

    lax.fori_loop(0, chunks // rows, add, 0)

    def power(base):
        return lax.fori_loop(
            0, step_ref[0], lambda i, p: p * base, jnp.full((1, LANES), 1.0, jnp.float32)
        )

    scales_ref[0:1, :] = 1.0 / (1.0 - power(jnp.float32(0.9)))
    scales_ref[1:2, :] = 1.0 / (1.0 - power(jnp.float32(0.999)))
    for copy in copies:
        copy.wait()
    squares[...] = weights_ref[...] * weights_ref[...]
    segment_rows(squares, table, bounds_ref)
    sums_ref[...] = jnp.pad(jnp.sum(table[...].T, axis=0, keepdims=True), ((0, 0), (0, LANES - table.shape[0])))


def update_kernel(n, bounds_ref, scales_ref, sums_ref, weights_ref, moment1_ref, moment2_ref, *rest):
    partial_ref, pieces = rest[0], rest[1 : n + 1]
    rest = rest[1:]
    new1_ref, new2_ref, update_ref, send_ref = rest[n : n + 4]
    squares, table = rest[n + 4 :]

    scale1, scale2 = scales_ref[0:1, :], scales_ref[1:2, :]
    chunks = weights_ref.shape[0]
    rows = math.gcd(chunks, TILE)

    def block(t, carry):
        part = pl.ds(pl.multiple_of(t * rows, rows), rows)
        grad = partial_ref[part, :] + total_of(pieces, part)
        new1 = 0.9 * moment1_ref[part, :] + 0.1 * grad
        new2 = 0.999 * moment2_ref[part, :] + 0.001 * grad * grad
        new1_ref[part, :] = new1
        new2_ref[part, :] = new2
        update = (new1 * scale1) / (jnp.sqrt(new2 * scale2) + 1e-06)
        update = update + 0.1 * weights_ref[part, :]
        update_ref[part, :] = update
        squares[part, :] = update * update
        return carry

    lax.fori_loop(0, chunks // rows, block, 0, unroll=2)
    segment_rows(squares, table, bounds_ref)
    mine = jnp.pad(jnp.sum(table[...].T, axis=0, keepdims=True), ((0, 0), (0, LANES - table.shape[0])))
    half = (send_ref.shape[0], LANES)
    send_ref[:, :LANES] = jnp.broadcast_to(sums_ref[...], half)
    send_ref[:, LANES:] = jnp.broadcast_to(mine, half)


def scaled(bounds, table, weights, update, write):
    chunks = weights.shape[0]
    rows = math.gcd(chunks, TILE)
    size = rows * LANES
    place = places(rows)
    count = bounds.shape[0] - 3

    def segment(k, carry):
        low, high = bounds[k], bounds[k + 1]
        scale = table[pl.ds(k, 1), :]

        def step(t, carry):
            part = pl.ds(pl.multiple_of(t * rows, rows), rows)
            new = weights[part, :] - scale * update[part, :]
            write(part, place >= low - t * size, new)
            return carry

        return lax.fori_loop(low // size, (high + (size - 1)) // size, step, carry)

    lax.fori_loop(bounds[count + 1], bounds[count + 2], segment, 0)


def narrow_kernel(bounds_ref, sums_ref, weights_ref, update_ref, narrow_ref, table):
    both = jnp.sum(sums_ref[...], axis=0, keepdims=True)
    ratio = jnp.sqrt(both[:, :LANES]) / jnp.maximum(jnp.sqrt(both[:, LANES:]), 1.0)
    ratio = 0.25 * ratio
    table[...] = jnp.broadcast_to(ratio, (LANES, LANES)).T[: table.shape[0], :]

    def write(part, mine, new):
        new = jnp.where(mine, new, narrow_ref[part, :].astype(jnp.float32))
        narrow_ref[part, :] = new.astype(jnp.bfloat16)

    scaled(bounds_ref, table, weights_ref, update_ref, write)


def store_kernel(bounds_ref, table, weights_ref, update_ref, new1_ref, new2_ref, *rest):
    out1_ref, out2_ref, out_ref, new_ref, sems = rest
    pairs = ((new1_ref, out1_ref), (new2_ref, out2_ref), (new_ref, out_ref))
    copies = [pltpu.make_async_copy(*pair, sems.at[i]) for i, pair in enumerate(pairs)]
    copies[0].start()
    copies[1].start()

    def write(part, mine, new):
        new_ref[part, :] = jnp.where(mine, new, new_ref[part, :])

    scaled(bounds_ref, table, weights_ref, update_ref, write)
    copies[2].start()
    for copy in copies:
        copy.wait()


def exchange_order(n):
    first = [k for k in ORDER if k < n]
    return first + [k for k in range(1, n) if k not in first]


def swap(value, axis, size, k):
    return lax.ppermute(value, axis, [(i, i ^ k) for i in range(size)])


def local(step, lengths, grads, weights, moment1, moment2):
    n = lax.axis_size("shard")
    everyone = n * lax.axis_size("tensor")
    width = weights.shape[0]
    chunks = width // LANES
    count = lengths.shape[0]
    flat = lambda dtype: jax.ShapeDtypeStruct((chunks, LANES), dtype)
    rows = grads.reshape(n // 8, 8, chunks, LANES).transpose(0, 2, 1, 3)
    parts = math.gcd(PARTS, chunks // 16)
    depth = chunks // parts
    staging = [
        pltpu.VMEM((parts, n // 8, depth, 8, LANES), jnp.bfloat16),
        pltpu.VMEM((parts, n * depth, LANES), jnp.float32),
        pltpu.SemaphoreType.DMA((parts,)),
    ]
    pieces = pl.pallas_call(
        functools.partial(split_kernel, n, chunks),
        out_shape=[flat(jnp.bfloat16)] * n,
        in_specs=[HBM],
        out_specs=[VMEM] * n,
        scratch_shapes=staging,
        compiler_params=BIG,
        name="split",
    )(pltpu.with_memory_space_constraint(rows, pltpu.HBM))
    order = exchange_order(n)
    pieces = [pieces[0]] + [swap(pieces[k], "shard", n, k) for k in order]
    early, late = pieces[: EARLY + 1], pieces[EARLY + 1 :]
    square_table = [
        pltpu.VMEM((chunks, LANES), jnp.float32),
        pltpu.VMEM((-(-count // 16) * 16, LANES), jnp.float32),
    ]
    stored = [
        pltpu.with_memory_space_constraint(value.reshape(chunks, LANES), pltpu.HBM)
        for value in (weights, moment1, moment2)
    ]
    weights, moment1, moment2, partial, sums, scales, bounds = pl.pallas_call(
        functools.partial(early_kernel, len(early)),
        out_shape=[flat(jnp.float32)] * 4
        + [
            jax.ShapeDtypeStruct((1, LANES), jnp.float32),
            jax.ShapeDtypeStruct((2, LANES), jnp.float32),
            jax.ShapeDtypeStruct((count + 3,), jnp.int32),
        ],
        in_specs=[SMEM] * 2 + [HBM] * 3 + [VMEM] * len(early),
        out_specs=[VMEM] * 6 + [SMEM],
        scratch_shapes=square_table + [pltpu.SemaphoreType.DMA((3,))],
        compiler_params=BIG,
        cost_estimate=pl.CostEstimate(
            flops=8 * width, bytes_accessed=24 * width, transcendentals=0
        ),
        name="early",
    )(step, lengths, *stored, *early)
    new1, new2, update, send = pl.pallas_call(
        functools.partial(update_kernel, len(late)),
        out_shape=[flat(jnp.float32)] * 3
        + [jax.ShapeDtypeStruct((everyone, 2 * LANES), jnp.float32)],
        in_specs=[SMEM] + [VMEM] * (6 + len(late)),
        out_specs=[VMEM] * 4,
        scratch_shapes=square_table,
        compiler_params=BIG,
        name="update",
    )(bounds, scales, sums, weights, moment1, moment2, partial, *late)
    sums = lax.all_to_all(send, ("shard", "tensor"), 0, 0, tiled=True)
    narrow, table = pl.pallas_call(
        narrow_kernel,
        out_shape=[flat(jnp.bfloat16), jax.ShapeDtypeStruct((-(-count // 16) * 16, LANES), jnp.float32)],
        in_specs=[SMEM, VMEM, VMEM, VMEM],
        out_specs=[VMEM] * 2,
        compiler_params=BIG,
        name="narrow_weights",
    )(bounds, sums, weights, update)
    gathered = {0: narrow}
    for k in range(2, n, 2):
        gathered[k] = swap(narrow, "shard", n, k)
    new1, new2, new = pl.pallas_call(
        store_kernel,
        out_shape=[flat(jnp.float32)] * 3,
        in_specs=[SMEM] + [VMEM] * 5,
        out_specs=[HBM] * 3,
        scratch_shapes=[
            pltpu.VMEM((chunks, LANES), jnp.float32),
            pltpu.SemaphoreType.DMA((3,)),
        ],
        compiler_params=BIG,
        cost_estimate=pl.CostEstimate(
            flops=4 * width, bytes_accessed=20 * width, transcendentals=0
        ),
        name="store",
    )(bounds, table, weights, update, new1, new2)
    new1, new2, new, own = lax.optimization_barrier((new1, new2, new, narrow))
    gathered[1] = swap(own, "shard", n, 1)
    for k in range(2, n, 2):
        gathered[k + 1] = swap(gathered[k], "shard", n, 1)
    soon, last = [0, 1, *range(2, n, 2)], list(range(3, n, 2))
    wide = jax.ShapeDtypeStruct((parts, n * depth, LANES), jnp.float32)
    laid = pl.pallas_call(
        functools.partial(lay_kernel, soon),
        out_shape=wide,
        in_specs=[VMEM] * len(soon),
        out_specs=VMEM,
        compiler_params=BIG,
        cost_estimate=pl.CostEstimate(
            flops=0, bytes_accessed=6 * width * len(soon), transcendentals=0
        ),
        name="lay",
    )(*[gathered[k] for k in soon])
    joined, unused = pl.pallas_call(
        functools.partial(join_kernel, last),
        out_shape=[jax.ShapeDtypeStruct((n // 8, chunks, 8, LANES), jnp.bfloat16), wide],
        in_specs=[VMEM] * (1 + len(last)),
        out_specs=[HBM, VMEM],
        input_output_aliases={0: 1},
        scratch_shapes=[staging[0], staging[2]],
        compiler_params=BIG,
        name="join",
    )(laid, *[gathered[k] for k in last])
    train = joined.transpose(0, 2, 1, 3).reshape(n, 1, width)
    return (new.reshape(width), new1.reshape(width), new2.reshape(width), train)


def solution(mesh):
    whole = P(("shard", "tensor"))
    return jax.shard_map(
        local,
        mesh=mesh,
        in_specs=(P(), P(), P("shard", None, "tensor", None), whole, whole, whole),
        out_specs=(whole, whole, whole, P(None, "tensor", None)),
        check_vma=False,
    )
```
